128 devices in a mesh: doc: 8 (over x, core), term: 16 (over z, y).
Axes of the slice: x: 4, y: 4, z: 4, core: 2. Of those that a mesh axis runs over, the one named last changes fastest.
Arguments:
- query_states: bfloat16 [512, 32, 768], P('doc'), may hold values from -6 to 6
- token_ids: int32 [512, 32], P('doc'), may hold values from 0 to 30521, as said below
- transform_weight: bfloat16 [768, 768], replicated, may hold values from -0.21875 to 0.21875
- transform_bias: float32 [768], replicated, may hold values from -3 to 3
- norm_gain: float32 [768], replicated, may hold values from 0.5 to 1.5
- norm_bias: float32 [768], replicated, may hold values from -3 to 3
- decoder_weight: bfloat16 [768, 30720], P(None, 'term'), may hold values from -0.21875 to 0.21875
- decoder_bias: float32 [30720], P('term'), may hold values from -2.5 to 0.5
- candidates: int32 [512, 32], P('doc'), may hold values from 0 to 127, all different within a row; in each aligned block of 64 rows (0 to 63, 64 to 127, ...) at most 32 rows name the same one
- occupancy: int32 [128, 240], P('doc', 'term'), may hold values 0 or 1
- doc_blocks: bfloat16 [128, 240, 128, 128], P('doc', 'term'), may hold values from -0.046875 to 0.046875
Outputs:
- query_weights: bfloat16 [512, 30720], P('doc', 'term')
- scores: float32 [512, 32, 128], P('doc', None, 'term')
The draws below stay inside these ranges and needn't reach their ends.
Inputs may be any that keep to these rules, and one draw needn't show every extreme that they name: `token_ids`: id 0 marks padding: a query has non-zero ids at its first positions, at least 8 of them, and 0 after them. `candidates`: A query names 32 different tiles; among the 64 queries of one doc index no tile is named by more than 32 of them.
All inputs are finite; a program needn't handle non-finite values. No bound on the sum of `occupancy` on one device may be relied on, other than what follows from the above.
Results may differ from the reference program's by a relative error of at most 0.0041.
Values may be sent and summed in bfloat16 or wider, within the bound.
A program may use at most 128 MiB of HBM per device.

```python
import math
import jax
import jax.numpy as jnp
import numpy as np
from jax import lax

DM = 768
VOCAB = 30522
BS = 128
TB = 240
TILE = 128
Q_DEV = 64
QLEN = 32
CAND = 32
MOST = 32
VP = 30720
NT = 128
QUERIES = 512
N_DOC = 8


def draw_token_ids(key, part):
    length_key, token_key = jax.random.split(key)
    lengths = jax.random.randint(length_key, (QUERIES, 1), max(1, QLEN // 4), QLEN + 1)
    tokens = jax.random.randint(token_key, (QUERIES, QLEN), 1, VOCAB)
    position = lax.iota(jnp.int32, QLEN)[None, :]
    return jnp.where(position < lengths, tokens, 0).astype(jnp.int32)


def plant(array, key, least, top_value):
    longest = array.shape.index(max(array.shape))
    spots = []
    for shift in (0, 1):
        where = [jax.random.randint(jax.random.fold_in(key, axis), (), 0, length) for axis, length in enumerate(array.shape)]
        where[longest] = (where[longest] + shift) % array.shape[longest]
        spots.append(tuple(where))
    return array.at[spots[0]].set(least).at[spots[1]].set(top_value)


def with_spikes(values, stream_key, source, target, blocks, factor):
    owner, partner = [(jnp.arange(values.shape[dim]) // (values.shape[dim] // blocks)).reshape([-1 if axis == dim else 1 for axis in range(values.ndim)]) for dim in (source, target)]
    chosen = jax.random.permutation(stream_key, blocks)[partner]
    strong = (owner == chosen) | (owner == (partner + blocks // 2) % blocks)
    return jnp.where(strong, factor * values, values)


def block_scale(own_key, dims, pieces, smallest, top_value):
    gain, own = 1.0, jax.random.fold_in(own_key, 6)
    for dim, blocks in pieces:
        heights = jnp.exp(jax.random.uniform(jax.random.fold_in(own, dim), (blocks,), jnp.float32, smallest / len(pieces), top_value / len(pieces)))
        gain = gain * jnp.repeat(heights, dims[dim] // blocks).reshape([-1 if axis == dim else 1 for axis in range(len(dims))])
    return gain


def deal_out(stream_key, own, number, rows, count, top, reach, lean):
    sequence = jax.random.permutation(stream_key, count)
    heavy_load, ordinary = portions_of(count, rows * top, reach, lean, True), portions_of(count, rows * top, reach, lean, False)
    places = jnp.arange(count)

    def named(sizes, offset_by):
        used = int((sizes > 0).sum())
        fixed = max(1, used // 4)
        moved = fixed + (places - fixed + offset_by * (used - fixed)) % max(1, count - fixed)
        return jnp.zeros((count,), jnp.int32).at[sequence[jnp.where(places < fixed, places, moved)]].set(jnp.asarray(sizes, jnp.int32))

    sizes = jnp.where(number % 4 == 0, named(heavy_load, number // 4), named(ordinary, number - number // 4 - 1))
    mixed = jax.random.permutation(jax.random.fold_in(own, 3), count)
    source_of, taker = mixed[0:count // 2 * 2:2], mixed[1:count // 2 * 2:2]
    slack = jnp.minimum(sizes[source_of] - 1, reach - sizes[taker]) // 2
    slack = jnp.where((source_of == sequence[0]) | (taker == sequence[0]) | (sizes[taker] == 0), 0, jnp.maximum(slack, 0))
    moved = jax.random.randint(jax.random.fold_in(own, 4), (count // 2,), 0, 1 << 20) % (slack + 1)
    sizes = sizes.at[source_of].add(-moved).at[taker].add(moved)
    items = jnp.searchsorted(jnp.cumsum(sizes), jnp.arange(rows * top), side="right").astype(jnp.int32)
    table = items.reshape(top, rows).T
    table = table[jax.random.permutation(jax.random.fold_in(own, 1), rows)]
    offset_by = jax.random.randint(jax.random.fold_in(own, 2), (rows, 1), 0, top)
    return jnp.take_along_axis(table, (jnp.arange(top)[None, :] + offset_by) % top, axis=1)


def portions_of(count, total, limit, skew, full):
    portions = [(1 << 20) // math.isqrt(grade ** skew) + 1 for grade in range(1, count + 1)]
    largest = limit if full else min(limit, max(-(-total // count), total * portions[0] // sum(portions)))
    least = 1 if total - largest >= count - 1 else 0
    counts, rest = [largest] + [least] * (count - 1), total - largest - least * (count - 1)
    while rest > 0:
        free = [i for i in range(1, count) if counts[i] < largest] or [i for i in range(1, count) if counts[i] < limit]
        whole, remaining = sum([portions[i] for i in free]), rest
        for i in free:
            extra = min(limit - counts[i], max(1, remaining * portions[i] // whole), rest)
            counts[i] = counts[i] + extra
            rest = rest - extra
    return np.array(counts)


def gaussian(stream_key, dims, scale, most, cuts=(), kind=jnp.bfloat16):
    factor_of = block_scale(stream_key, dims, cuts, -0.22, 0.18) if cuts else 1.0
    entries = jax.random.normal(stream_key, dims, jnp.float32) * scale * factor_of
    return jnp.minimum(jnp.maximum(entries, -most), most).astype(kind)


def bell_draw_with(rng, shape, width, bound, cuts, heavy, dtype=jnp.bfloat16):
    result = width * jax.random.normal(rng, shape, jnp.float32)
    if cuts:
        result = result * block_scale(rng, shape, cuts, -0.22, 0.18)
    return jnp.clip(with_spikes(result, jax.random.fold_in(rng, 3), *heavy), -bound, bound).astype(dtype)


def setup_inputs(seed: int = 0) -> dict:
    seeds = jax.random.split(jax.random.key(seed), 12)
    query_states = gaussian(seeds[0], (QUERIES, QLEN, DM), 1.0, 6.0, ((0, 8),))
    token_ids = draw_token_ids(jax.random.fold_in(seeds[11], 71), 0)
    transform_weight = gaussian(seeds[2], (DM, DM), DM ** -0.5, 0.21875)
    transform_bias = gaussian(seeds[3], (DM,), 0.5, 3.0, (), jnp.float32)
    norm_gain = jnp.clip(1.0 + 0.1 * jax.random.normal(seeds[4], (DM,), jnp.float32), 0.5, 1.5)
    norm_bias = gaussian(seeds[5], (DM,), 0.5, 3.0, (), jnp.float32)
    decoder_weight = gaussian(seeds[6], (DM, VP), DM ** -0.5, 0.21875, ((1, 16),))
    decoder_bias = jnp.clip(-2.5 + 3.0 * jax.random.uniform(seeds[7], (VP,), jnp.float32) ** block_scale(seeds[7], (VP,), ((0, 16),), -0.2, 0.2), -2.5, 0.5)
    candidates_keys = jax.random.split(jax.random.fold_in(seeds[8], 1), QUERIES // Q_DEV)
    candidates_turns = jax.random.permutation(jax.random.fold_in(seeds[8], 3), QUERIES // Q_DEV)
    candidates = jax.vmap(lambda own, number: deal_out(jax.random.fold_in(seeds[8], 2), own, number, Q_DEV, NT, CAND, MOST, 2))(candidates_keys, candidates_turns).reshape((QUERIES, CAND))
    occupancy = plant((jax.random.randint(seeds[9], (NT, TB), 0, 4) < 3).astype(jnp.int32), jax.random.fold_in(seeds[9], 1), 0, 1)
    doc_blocks = bell_draw_with(seeds[10], (NT, TB, TILE, BS), VOCAB ** -0.5, 0.046875, ((0, 8), (1, 16)), (1, 2, 16, 2.0))
    return {"query_states": query_states, "token_ids": token_ids, "transform_weight": transform_weight, "transform_bias": transform_bias, "norm_gain": norm_gain, "norm_bias": norm_bias, "decoder_weight": decoder_weight, "decoder_bias": decoder_bias, "candidates": candidates, "occupancy": occupancy, "doc_blocks": doc_blocks}


def expand(states, token_mask, transform_weight, transform_bias, norm_gain, norm_bias, decoder_weight, decoder_bias):
    query_count, query_length, model_width = states.shape
    hidden = jnp.dot(states.reshape(query_count * query_length, model_width), transform_weight, preferred_element_type=jnp.float32) + transform_bias
    hidden = jax.nn.gelu(hidden, approximate=False)
    centred = hidden - lax.optimization_barrier(jnp.mean(hidden, axis=-1, keepdims=True))
    spread = lax.optimization_barrier(jnp.mean(centred * centred, axis=-1, keepdims=True))
    normed = (centred * lax.rsqrt(spread + 1e-06) * norm_gain + norm_bias).astype(jnp.bfloat16)
    logits = jnp.dot(normed, decoder_weight, preferred_element_type=jnp.float32) + decoder_bias
    activated = jnp.log1p(jnp.maximum(logits, 0.0)).reshape(query_count, query_length, -1)
    live_mask = (token_mask != 0).astype(jnp.float32)[:, :, None]
    return lax.optimization_barrier(jnp.max(activated * live_mask, axis=1))

def reference(query_states, token_ids, transform_weight, transform_bias, norm_gain, norm_bias, decoder_weight, decoder_bias, candidates, occupancy, doc_blocks):
    state_blocks = query_states.reshape(N_DOC, Q_DEV, QLEN, DM)
    id_blocks = token_ids.reshape(N_DOC, Q_DEV, QLEN)

    def expand_block(packed):
        return expand(packed[0], packed[1], transform_weight, transform_bias, norm_gain, norm_bias, decoder_weight, decoder_bias)
    pooled = lax.map(expand_block, (state_blocks, id_blocks)).reshape(QUERIES, VP)
    vocab_keep = (lax.iota(jnp.int32, VP) < VOCAB).astype(jnp.float32)
    weights = (pooled * vocab_keep).astype(jnp.bfloat16)
    tile_index = lax.iota(jnp.int32, NT)
    tile_hits = lax.optimization_barrier(jnp.sum((candidates[:, :, None] == tile_index[None, None, :]).astype(jnp.int32), axis=1)).reshape(N_DOC, Q_DEV, NT)
    tile_before = jnp.cumsum(tile_hits, axis=1) - tile_hits
    hits_by_tile = jnp.transpose(tile_hits, (2, 0, 1))
    before_by_tile = jnp.transpose(tile_before, (2, 0, 1))
    slot_index = lax.iota(jnp.int32, MOST)
    row_index = lax.iota(jnp.int32, Q_DEV)
    block_start = lax.iota(jnp.int32, N_DOC)[:, None] * Q_DEV

    def tile_scores(packed):
        one_hits, one_before, one_block, one_occupied = packed
        chosen = (one_hits[:, None, :] > 0) & (one_before[:, None, :] == slot_index[None, :, None])
        source_row = lax.optimization_barrier(jnp.sum(jnp.where(chosen, row_index[None, None, :], 0), axis=-1))
        slot_valid = jnp.any(chosen, axis=-1).astype(jnp.float32)
        flat_index = (block_start + source_row).reshape(-1)
        gathered = jnp.take(weights, flat_index, axis=0).astype(jnp.float32).reshape(N_DOC, MOST, TB, BS)
        gathered = gathered * slot_valid[:, :, None, None] * one_occupied.astype(jnp.float32)[None, None, :, None]
        return jnp.einsum('jrbc,bdc->jrd', gathered, one_block.astype(jnp.float32), precision=lax.Precision.HIGHEST)
    table = lax.map(tile_scores, (hits_by_tile, before_by_tile, doc_blocks, occupancy))
    slot_rank = jnp.take_along_axis(tile_before.reshape(QUERIES, NT), candidates, axis=1)
    owner = (lax.iota(jnp.int32, QUERIES) // Q_DEV)[:, None]
    flat_index = (candidates * N_DOC + owner) * MOST + slot_rank
    scores = jnp.take(table.reshape(-1, TILE), flat_index.reshape(-1), axis=0).reshape(QUERIES, CAND, TILE)
    return (weights, scores)
```

```python
import jax
import jax.numpy as jnp
from jax import lax
from jax.experimental import pallas as pl
from jax.experimental.pallas import tpu as pltpu
from jax.sharding import PartitionSpec as P

MESH = pl.DeviceIdType.MESH
VOCAB = 30522
NDOC = 8
NY = 4
NZ = 4
QD = 64
QLEN = 32
DM = 768
VL = 1920
NB = 15
NTL = 16
CAND = 32
CH = 16
TOK = CH * QLEN
HQ = 32
HL = NDOC * HQ
COLS = 384
BF = jnp.bfloat16
F32 = jnp.float32


def kernel(
    x_hbm, tok_ref, tw_hbm, tb_ref, g_ref, nb_ref, dw_hbm, db_ref, cand_ref, occ_ref, docs_hbm,
    qw_ref, out_ref,
    xv, twv, dwv, dv, occrow, lens, nrm, wall, wt, sbuf, rbuf, s2buf, r2buf, pbuf, back,
    xsem, wsem, dsem, ag_s, ag_r, s1_s, s1_r, s2_s, s2_r, rt_s, rt_r,
):
    doc = lax.axis_index("doc")
    term = lax.axis_index("term")
    z = term // NY
    y = lax.rem(term, NY)

    tw_cp = pltpu.make_async_copy(tw_hbm, twv, wsem.at[0])
    tw_cp.start()
    dw_cp = pltpu.make_async_copy(dw_hbm, dwv, wsem.at[1])

    def x_copy(c):
        return pltpu.make_async_copy(x_hbm.at[pl.ds(c * CH, CH)], xv.at[pl.ds(c * CH, CH)], xsem.at[c])

    def d_copy(b):
        return pltpu.make_async_copy(docs_hbm.at[:, b], dv.at[:, :, pl.ds(b * 128, 128)], dsem.at[b])

    x_copy(0).start()
    dw_cp.start()
    for c in range(1, 4):
        x_copy(c).start()
    for b in range(NB):
        d_copy(b).start()

    barrier = pltpu.get_barrier_semaphore()
    for k in range(1, NDOC):
        pl.semaphore_signal(barrier, inc=1, device_id={"doc": lax.rem(doc + k, NDOC)}, device_id_type=MESH)
    for k in range(1, 4):
        pl.semaphore_signal(barrier, inc=1, device_id={"term": z * NY + lax.rem(y + k, NY)}, device_id_type=MESH)
        pl.semaphore_signal(barrier, inc=1, device_id={"term": lax.rem(z + k, NZ) * NY + y}, device_id_type=MESH)

    live = jnp.where(tok_ref[...] != 0, 1.0, 0.0).astype(BF)
    lens[...] = lax.dot_general(
        live, jnp.ones((QLEN, DM), BF), (((0,), (0,)), ((), ())), preferred_element_type=F32
    )
    spread = jnp.where(
        lax.broadcasted_iota(jnp.int32, (NB, VL), 1) // 128 == lax.broadcasted_iota(jnp.int32, (NB, VL), 0), 1.0, 0.0
    ).astype(BF)
    occrow[...] = jnp.dot(occ_ref[...].astype(F32).astype(BF), spread, preferred_element_type=F32)

    def ag_copy(c, k):
        half, sub = c // 2, lax.rem(c, 2)
        place = wall.at[half, doc, pl.ds(sub * CH, CH)]
        return pltpu.make_async_remote_copy(
            src_ref=place, dst_ref=place, send_sem=ag_s.at[c, k], recv_sem=ag_r.at[c, k],
            device_id={"doc": lax.rem(doc + k + 1, NDOC)}, device_id_type=MESH,
        )

    def expand(c):
        x_copy(c).wait()
        rows = pl.ds(pl.multiple_of(c * CH, CH), CH)
        h = jnp.dot(xv[rows].reshape(TOK, DM), twv[...], preferred_element_type=F32) + tb_ref[...]
        h = 0.5 * h * (1.0 + lax.erf(h * 0.7071067811865476))
        cen = h - jnp.mean(h, axis=-1, keepdims=True)
        var = jnp.mean(cen * cen, axis=-1, keepdims=True)
        n = cen * lax.rsqrt(var + 1e-6) * g_ref[...] + nb_ref[...]
        n3 = n.reshape(CH, QLEN, DM)
        pos = lax.broadcasted_iota(jnp.int32, (CH, QLEN, DM), 1).astype(F32)
        n3 = jnp.where(pos < lens[rows, :][:, None, :], n3, n3[:, 0:1, :])
        nrm[...] = n3.reshape(TOK, DM).astype(BF)

    def decode(c):
        half, sub = c // 2, lax.rem(c, 2)
        rows = pl.ds(pl.multiple_of(c * CH, CH), CH)
        srow = pl.ds(pl.multiple_of(sub * CH, CH), CH)
        for c0 in range(0, VL, COLS):
            lg = jnp.dot(nrm[...], dwv[:, c0:c0 + COLS], preferred_element_type=F32)
            top = jnp.max(lg.reshape(CH, QLEN, COLS), axis=1) + db_ref[:, c0:c0 + COLS]
            w = jnp.log1p(jnp.maximum(top, 0.0))
            col = term * VL + c0 + lax.broadcasted_iota(jnp.int32, (CH, COLS), 1)
            w = jnp.where(col < VOCAB, w, 0.0).astype(BF)
            wall[half, doc, srow, c0:c0 + COLS] = w
            qw_ref[rows, c0:c0 + COLS] = w

    def ag_start(c):
        for k in range(NDOC - 1):
            ag_copy(c, k).start()

    def ag_wait(c):
        for k in range(NDOC - 1):
            ag_copy(c, k).wait_recv()

    def s1_copy(half, g, k, y_first):
        if y_first:
            peer = lax.rem(y + k + 1, NY)
            to = {"term": z * NY + peer}
        else:
            peer = lax.rem(z + k + 1, NZ)
            to = {"term": peer * NY + y}
        return pltpu.make_async_remote_copy(
            src_ref=sbuf.at[half, g, peer], dst_ref=rbuf.at[half, g, k],
            send_sem=s1_s.at[half, g, k], recv_sem=s1_r.at[half, g, k], device_id=to, device_id_type=MESH,
        )

    def s2_copy(half, g, k, y_first):
        if y_first:
            peer = lax.rem(z + k + 1, NZ)
            to = {"term": peer * NY + y}
        else:
            peer = lax.rem(y + k + 1, NY)
            to = {"term": z * NY + peer}
        return pltpu.make_async_remote_copy(
            src_ref=s2buf.at[half, g, peer], dst_ref=r2buf.at[half, g, k],
            send_sem=s2_s.at[half, g, k], recv_sem=s2_r.at[half, g, k], device_id=to, device_id_type=MESH,
        )

    def rt_copy(half, k):
        peer = lax.rem(doc + k + 1, NDOC)
        return pltpu.make_async_remote_copy(
            src_ref=pbuf.at[half, peer], dst_ref=back.at[half, doc],
            send_sem=rt_s.at[half, k], recv_sem=rt_r.at[half, k], device_id={"doc": peer}, device_id_type=MESH,
        )

    def mask_docs(g):
        for t in range(4):
            tile = g * 4 + t
            row = occrow[pl.ds(tile, 1), :].astype(BF)
            dv[tile] = dv[tile] * row

    def score(half):
        for c0 in range(0, VL, 128):
            part = wall[half, :, :, c0:c0 + 128].reshape(HL, 128)
            wt[c0:c0 + 128, :] = part.T

        for y_first in (True, False):
            @pl.loop(0, 2)
            def _(i):
                g = i if y_first else i + 2
                if half == 0:
                    mask_docs(g)
                docs = dv[pl.ds(g * 4, 4)].reshape(512, VL)
                r = jnp.dot(docs, wt[...], preferred_element_type=F32).reshape(4, NZ, NY, 8, HL)
                for zz in range(NZ):
                    for yy in range(NY):
                        part = jnp.concatenate([r[t, zz, yy] for t in range(4)], axis=0).astype(BF)
                        slot, at = (yy, zz) if y_first else (zz, yy)
                        sbuf[half, g, slot, at * 32:(at + 1) * 32, :] = part
                for k in range(3):
                    s1_copy(half, g, k, y_first).start()

    def reduce1(half):
        for g in range(4):
            y_first = g < 2
            for k in range(3):
                s1_copy(half, g, k, y_first).wait_recv()
            tot = sbuf[half, g, y if y_first else z].astype(F32)
            for k in range(3):
                tot = tot + rbuf[half, g, k].astype(F32)
            s2buf[half, g] = tot.astype(BF).reshape(4, 32, HL)
            for k in range(3):
                s2_copy(half, g, k, y_first).start()

    def reduce2(half):
        lane_group = lax.broadcasted_iota(jnp.int32, (8, 128), 1) // HQ
        for g in range(4):
            y_first = g < 2
            for k in range(3):
                s2_copy(half, g, k, y_first).wait_recv()
            tot = s2buf[half, g, z if y_first else y].astype(F32)
            for k in range(3):
                tot = tot + r2buf[half, g, k].astype(F32)
            for j in range(NDOC):
                made = jnp.zeros((8, 128), F32)
                for t in range(4):
                    piece = tot[t * 8:(t + 1) * 8, (j // 4) * 128:(j // 4 + 1) * 128]
                    turn = ((t - j % 4) * HQ) % 128
                    if turn:
                        piece = pltpu.roll(piece, turn, 1)
                    made = jnp.where(lane_group == t, piece, made)
                pbuf[half, j, g] = made
        for k in range(NDOC - 1):
            rt_copy(half, k).start()
        back[half, doc] = pbuf[half, doc]

    def select(half):
        for k in range(NDOC - 1):
            rt_copy(half, k).wait_recv()
        part = lax.broadcasted_iota(jnp.int32, (8, 128), 1) // HQ
        for c in range(CAND):
            row = cand_ref[half, c:c + 1, :]
            want = jnp.broadcast_to(row, (8, 128)) - part
            acc = jnp.zeros((8, 128), F32)
            for d in range(NDOC):
                for g in range(4):
                    acc = jnp.where(want == d * 16 + g * 4, back[half, d, g], acc)
            acc = acc + pltpu.roll(acc, 64, 1)
            acc = acc + pltpu.roll(acc, 32, 1)
            out_ref[c, :, half * HQ:(half + 1) * HQ] = acc[:, 0:HQ]

    tw_cp.wait()
    expand(0)
    dw_cp.wait()
    decode(0)
    pl.semaphore_wait(barrier, NDOC - 1 + 6)
    ag_start(0)

    @pl.loop(1, 3)
    def _(c):
        expand(c)
        decode(c)
        ag_start(c)

    for b in range(NB):
        d_copy(b).wait()
    ag_wait(0)
    ag_wait(1)
    score(0)
    expand(3)
    decode(3)
    ag_start(3)
    reduce1(0)
    ag_wait(2)
    ag_wait(3)
    score(1)
    reduce2(0)
    reduce1(1)
    select(0)
    reduce2(1)
    select(1)

    for c in range(4):
        for k in range(NDOC - 1):
            ag_copy(c, k).wait_send()
    for half in range(2):
        for g in range(4):
            for k in range(3):
                s1_copy(half, g, k, g < 2).wait_send()
                s2_copy(half, g, k, g < 2).wait_send()
        for k in range(NDOC - 1):
            rt_copy(half, k).wait_send()


def body(
    query_states, token_ids, transform_weight, transform_bias, norm_gain, norm_bias,
    decoder_weight, decoder_bias, candidates, occupancy, doc_blocks,
):
    cand = candidates.T.reshape(CAND, 2, 1, HQ)
    cand = jnp.broadcast_to(cand, (CAND, 2, 4, HQ)).transpose(1, 0, 2, 3).reshape(2, CAND, 128)
    any_ = pl.BlockSpec(memory_space=pl.ANY)
    vm = pl.BlockSpec(memory_space=pltpu.VMEM)
    dma = pltpu.SemaphoreType.DMA
    weights, picked = pl.pallas_call(
        kernel,
        out_shape=(
            jax.ShapeDtypeStruct((QD, VL), BF),
            jax.ShapeDtypeStruct((CAND, 8, QD), F32),
        ),
        in_specs=[any_, vm, any_, vm, vm, vm, any_, vm, vm, vm, any_],
        out_specs=(vm, vm),
        scratch_shapes=[
            pltpu.VMEM((QD, QLEN, DM), BF),
            pltpu.VMEM((DM, DM), BF),
            pltpu.VMEM((DM, VL), BF),
            pltpu.VMEM((NTL, 128, VL), BF),
            pltpu.VMEM((NTL, VL), F32),
            pltpu.VMEM((QD, DM), F32),
            pltpu.VMEM((TOK, DM), BF),
            pltpu.VMEM((2, NDOC, HQ, VL), BF),
            pltpu.VMEM((VL, HL), BF),
            pltpu.VMEM((2, 4, 4, 128, HL), BF),
            pltpu.VMEM((2, 4, 3, 128, HL), BF),
            pltpu.VMEM((2, 4, 4, 32, HL), BF),
            pltpu.VMEM((2, 4, 3, 32, HL), BF),
            pltpu.VMEM((2, NDOC, 4, 8, 128), F32),
            pltpu.VMEM((2, NDOC, 4, 8, 128), F32),
            dma((4,)),
            dma((2,)),
            dma((NB,)),
            dma((4, NDOC - 1)),
            dma((4, NDOC - 1)),
            dma((2, 4, 3)),
            dma((2, 4, 3)),
            dma((2, 4, 3)),
            dma((2, 4, 3)),
            dma((2, NDOC - 1)),
            dma((2, NDOC - 1)),
        ],
        compiler_params=pltpu.CompilerParams(
            collective_id=0, has_side_effects=True, vmem_limit_bytes=56 * 1024 * 1024
        ),
        name="splade",
    )(
        query_states, token_ids.T, transform_weight, transform_bias.reshape(1, DM), norm_gain.reshape(1, DM),
        norm_bias.reshape(1, DM), decoder_weight, decoder_bias.reshape(1, VL), cand, occupancy, doc_blocks,
    )
    return weights, picked.transpose(2, 0, 1)


def solution(mesh):
    placed = (
        P("doc", None, None),
        P("doc", None),
        P(),
        P(),
        P(),
        P(),
        P(None, "term"),
        P("term"),
        P("doc", None),
        P("doc", "term"),
        P("doc", "term", None, None),
    )
    return jax.shard_map(
        body,
        mesh=mesh,
        in_specs=placed,
        out_specs=(P("doc", "term"), P("doc", None, "term")),
        check_vma=False,
    )
```

```python
import jax
import jax.numpy as jnp
from jax import lax
from jax.experimental import pallas as pl
from jax.experimental.pallas import tpu as pltpu
from jax.sharding import PartitionSpec as P

MESH = pl.DeviceIdType.MESH
VOCAB = 30522
NDOC = 8
NY = 4
NZ = 4
QD = 64
QLEN = 32
DM = 768
VL = 1920
NB = 15
NTL = 16
CAND = 32
CH = 16
TOK = CH * QLEN
HQ = 32
HL = NDOC * HQ
BLOCKS = ((0, 512), (512, 512), (1024, 512), (1536, 384))
PARTS = ((0, 1024), (1024, 896))
BF = jnp.bfloat16
F32 = jnp.float32


def kernel(
    x_hbm, tok_hbm, tw_hbm, tb_hbm, g_hbm, nb_hbm, dw_hbm, db_hbm, occ_hbm, docs_hbm,
    qw_ref, back,
    xv, twv, dwv, dv, tok_ref, tb_ref, g_ref, nb_ref, db_ref, occ_ref,
    occrow, lens, nrm, qw_v, wall, wt, sbuf, rbuf, s2buf, r2buf, pbuf,
    xsem, wsem, dsem, vsem, osem, ag_s, ag_r, ps_s, ps_r, s1_s, s1_r, s2_s, s2_r, rt_s, rt_r,
):
    doc = lax.axis_index("doc")
    term = lax.axis_index("term")
    z = term // NY
    y = lax.rem(term, NY)

    tw_cp = pltpu.make_async_copy(tw_hbm, twv, wsem.at[0])

    def dw_copy(i):
        cols = pl.ds(*BLOCKS[i])
        return pltpu.make_async_copy(dw_hbm.at[:, cols], dwv.at[:, cols], wsem.at[1 + i])

    def x_copy(c):
        return pltpu.make_async_copy(x_hbm.at[pl.ds(c * CH, CH)], xv.at[pl.ds(c * CH, CH)], xsem.at[c])

    def d_copy(b):
        return pltpu.make_async_copy(docs_hbm.at[:, b], dv.at[:, :, pl.ds(b * 128, 128)], dsem.at[b])

    small = [
        pltpu.make_async_copy(a, b, vsem.at[n])
        for n, (a, b) in enumerate((
            (tok_hbm, tok_ref), (tb_hbm, tb_ref), (g_hbm, g_ref), (nb_hbm, nb_ref), (db_hbm, db_ref), (occ_hbm, occ_ref),
        ))
    ]
    tw_cp.start()
    x_copy(0).start()
    for cp in small:
        cp.start()
    for i in range(len(BLOCKS)):
        dw_copy(i).start()
    for c in range(1, 4):
        x_copy(c).start()
    for b in range(NB):
        d_copy(b).start()

    barrier = pltpu.get_barrier_semaphore()
    for k in range(1, NDOC):
        pl.semaphore_signal(barrier, inc=1, device_id={"doc": lax.rem(doc + k, NDOC)}, device_id_type=MESH)
    for k in range(1, 4):
        pl.semaphore_signal(barrier, inc=1, device_id={"term": z * NY + lax.rem(y + k, NY)}, device_id_type=MESH)
        pl.semaphore_signal(barrier, inc=1, device_id={"term": lax.rem(z + k, NZ) * NY + y}, device_id_type=MESH)

    for cp in small:
        cp.wait()

    live = jnp.where(tok_ref[...] != 0, 1.0, 0.0).astype(BF)
    lens[...] = lax.dot_general(
        live, jnp.ones((QLEN, 128), BF), (((0,), (0,)), ((), ())), preferred_element_type=F32
    )
    spread = jnp.where(
        lax.broadcasted_iota(jnp.int32, (NB, VL), 1) // 128 == lax.broadcasted_iota(jnp.int32, (NB, VL), 0), 1.0, 0.0
    ).astype(BF)
    occrow[...] = jnp.dot(occ_ref[...].astype(F32).astype(BF), spread, preferred_element_type=F32)

    def row(ref):
        return jnp.concatenate([ref[i:i + 1, :] for i in range(ref.shape[0])], axis=1)

    tb, gain, nbias, dbias = row(tb_ref), row(g_ref), row(nb_ref), row(db_ref)
    sibling = doc + 1 - 2 * lax.rem(doc, 2)

    def ag_copy(c, k, part):
        half, sub = c // 2, lax.rem(c, 2)
        place = wall.at[half, doc, pl.ds(sub * CH, CH), pl.ds(*PARTS[part])]
        return pltpu.make_async_remote_copy(
            src_ref=place, dst_ref=place, send_sem=ag_s.at[c, k, part], recv_sem=ag_r.at[c, k, part],
            device_id={"doc": sibling if k == 0 else lax.rem(doc + 2 * k, NDOC)}, device_id_type=MESH,
        )

    def pass_copy(c, k):
        half, sub = c // 2, lax.rem(c, 2)
        place = wall.at[half, lax.rem(doc + NDOC - 2 * k, NDOC), pl.ds(sub * CH, CH)]
        return pltpu.make_async_remote_copy(
            src_ref=place, dst_ref=place, send_sem=ps_s.at[c, k - 1], recv_sem=ps_r.at[c, k - 1],
            device_id={"doc": sibling}, device_id_type=MESH,
        )

    def expand(c):
        x_copy(c).wait()
        rows = pl.ds(pl.multiple_of(c * CH, CH), CH)
        h = jnp.dot(xv[rows].reshape(TOK, DM), twv[...], preferred_element_type=F32) + tb
        h = 0.5 * h * (1.0 + lax.erf(h * 0.7071067811865476))
        cen = h - jnp.mean(h, axis=-1, keepdims=True)
        var = jnp.mean(cen * cen, axis=-1, keepdims=True)
        n = cen * lax.rsqrt(var + 1e-6) * gain + nbias
        n3 = n.reshape(CH, QLEN, DM)
        pos = lax.broadcasted_iota(jnp.int32, (CH, QLEN, DM), 1).astype(F32)
        length = jnp.concatenate([lens[rows, :]] * (DM // 128), axis=1)
        n3 = jnp.where(pos < length[:, None, :], n3, n3[:, 0:1, :])
        nrm[...] = n3.reshape(TOK, DM).astype(BF)

    def decode(c):
        half, sub = c // 2, lax.rem(c, 2)
        rows = pl.ds(pl.multiple_of(c * CH, CH), CH)
        srow = pl.ds(pl.multiple_of(sub * CH, CH), CH)
        for c0, COLS in BLOCKS:
            lg = jnp.dot(nrm[...], dwv[:, c0:c0 + COLS], preferred_element_type=F32)
            top = jnp.max(lg.reshape(CH, QLEN, COLS), axis=1) + dbias[:, c0:c0 + COLS]
            w = jnp.log1p(jnp.maximum(top, 0.0))
            col = term * VL + c0 + lax.broadcasted_iota(jnp.int32, (CH, COLS), 1)
            w = jnp.where(col < VOCAB, w, 0.0).astype(BF)
            wall[half, doc, srow, c0:c0 + COLS] = w
            qw_v[rows, c0:c0 + COLS] = w
            for part, (p0, width) in enumerate(PARTS):
                if c0 + COLS == p0 + width:
                    for k in (2, 1, 3, 0):
                        ag_copy(c, k, part).start()

    def ag_pass(c):
        for k in (1, 3, 2):
            for part in range(2):
                ag_copy(c, k, part).wait_recv()
            pass_copy(c, k).start()

    def ag_wait(c):
        for part in range(2):
            ag_copy(c, 0, part).wait_recv()
        for k in (1, 3, 2):
            pass_copy(c, k).wait_recv()

    def ag_sent(c):
        for k in range(4):
            for part in range(2):
                ag_copy(c, k, part).wait_send()
        for k in (1, 3, 2):
            pass_copy(c, k).wait_send()

    def peers(k):
        py = lax.rem(y + k + 1, NY)
        pz = lax.rem(z + k + 1, NZ)
        return (py, {"term": z * NY + py}), (pz, {"term": pz * NY + y})

    def s1_copy(half, axis, i, k):
        peer, to = peers(k)[axis]
        return pltpu.make_async_remote_copy(
            src_ref=sbuf.at[half, axis, i, peer], dst_ref=rbuf.at[half, axis, i, k],
            send_sem=s1_s.at[half, axis, i, k], recv_sem=s1_r.at[half, axis, i, k], device_id=to, device_id_type=MESH,
        )

    def s2_copy(half, axis, i, k):
        peer, to = peers(k)[1 - axis]
        return pltpu.make_async_remote_copy(
            src_ref=s2buf.at[half, axis, i, peer], dst_ref=r2buf.at[half, axis, i, k],
            send_sem=s2_s.at[half, axis, i, k], recv_sem=s2_r.at[half, axis, i, k], device_id=to, device_id_type=MESH,
        )


    def rt_copy(half, k):
        peer = lax.rem(doc + k + 1, NDOC)
        return pltpu.make_async_remote_copy(
            src_ref=pbuf.at[half, peer], dst_ref=back.at[half, doc],
            send_sem=rt_s.at[half, k], recv_sem=rt_r.at[half, k], device_id={"doc": peer}, device_id_type=MESH,
        )

    def own_copy(half):
        return pltpu.make_async_copy(pbuf.at[half, doc], back.at[half, doc], osem.at[half])

    def give_back(half):
        for k in range(NDOC - 1):
            rt_copy(half, k).start()
        own_copy(half).start()

    def score(half, masked, between):
        for c0 in range(0, VL, 128):
            part = wall[half, :, :, c0:c0 + 128].reshape(HL, 128)
            wt[c0:c0 + 128, :] = part.T

        @pl.loop(0, 2)
        def _(i):
            for axis in range(2):
                first = pl.multiple_of((2 * i + axis) * 4, 4)
                if masked:
                    for t in range(4):
                        keep = occrow[pl.ds(first + t, 1), :].astype(BF)
                        dv[first + t] = dv[first + t] * keep
                docs = dv[pl.ds(first, 4)].reshape(512, VL)
                r = jnp.dot(docs, wt[...], preferred_element_type=F32).reshape(4, NZ, NY, 8, HL)
                for zz in range(NZ):
                    for yy in range(NY):
                        part = jnp.concatenate([r[t, zz, yy] for t in range(4)], axis=0).astype(BF)
                        slot, at = (yy, zz) if axis == 0 else (zz, yy)
                        sbuf[half, axis, i, slot, at] = part
                for k in (1, 0, 2):
                    s1_copy(half, axis, i, k).start()
            if between is not None:
                @pl.when(i == 0)
                def _():
                    between()

    def reduce1(half, i, axis):
        for k in (0, 2, 1):
            s1_copy(half, axis, i, k).wait_recv()
        tot = sbuf[half, axis, i, y if axis == 0 else z].astype(F32)
        for k in range(3):
            tot = tot + rbuf[half, axis, i, k].astype(F32)
        s2buf[half, axis, i] = tot.astype(BF)
        for k in (1, 0, 2):
            s2_copy(half, axis, i, k).start()

    def reduce2(half, i, axis):
        lane_group = lax.broadcasted_iota(jnp.int32, (8, 128), 1) // HQ
        for k in (0, 2, 1):
            s2_copy(half, axis, i, k).wait_recv()
        tot = s2buf[half, axis, i, z if axis == 0 else y].astype(F32)
        for k in range(3):
            tot = tot + r2buf[half, axis, i, k].astype(F32)
        for j in range(NDOC):
            made = jnp.zeros((8, 128), F32)
            for t in range(4):
                piece = tot[t * 8:(t + 1) * 8, (j // 4) * 128:(j // 4 + 1) * 128]
                turn = ((t - j % 4) * HQ) % 128
                if turn:
                    piece = pltpu.roll(piece, turn, 1)
                made = jnp.where(lane_group == t, piece, made)
            pbuf[half, j, 2 * i + axis] = made

    tw_cp.wait()

    @pl.loop(0, 4)
    def _(c):
        expand(c)

        @pl.when(c == 0)
        def _():
            for i in range(len(BLOCKS)):
                dw_copy(i).wait()
            pl.semaphore_wait(barrier, NDOC - 1 + 6)

        @pl.when(c >= 2)
        def _():
            ag_pass(c - 2)

        decode(c)

    qw_cp = pltpu.make_async_copy(qw_v, qw_ref, osem.at[2])
    qw_cp.start()
    for b in range(NB):
        d_copy(b).wait()
    ag_wait(0)
    ag_wait(1)
    score(0, True, lambda: ag_pass(2))
    ag_pass(3)
    for c in range(3):
        ag_sent(c)
    ag_wait(2)
    ag_wait(3)
    score(1, False, None)
    ag_sent(3)
    groups = [(half, i, axis) for half in range(2) for i in range(2) for axis in range(2)]
    for group in groups:
        reduce1(*group)
    for half, i, axis in groups:
        for k in range(3):
            s1_copy(half, axis, i, k).wait_send()
    for n, group in enumerate(groups):
        reduce2(*group)
        if n in (3, 7):
            give_back(n // 4)
    for half, i, axis in groups:
        for k in range(3):
            s2_copy(half, axis, i, k).wait_send()
    qw_cp.wait()
    for half in range(2):
        own_copy(half).wait()
        for k in range(NDOC - 1):
            rt_copy(half, k).wait()


def pick(qw_ref, back, cand_ref, qw_out, out_ref, want):
    qw_out[...] = qw_ref[...]
    part = lax.broadcasted_iota(jnp.int32, (CAND, 128), 1) // HQ
    for half in range(2):
        mine = cand_ref[:, half * HQ:(half + 1) * HQ]
        want[half] = jnp.concatenate([mine] * 4, axis=1) - part

    @pl.loop(0, CAND // 8)
    def _(block):
        made = []
        for half in range(2):
            rows = want[half, pl.ds(pl.multiple_of(block * 8, 8), 8), :]
            each = [jnp.broadcast_to(rows[i:i + 1, :], (8, 128)) for i in range(8)]
            accs = [jnp.zeros((8, 128), F32) for _ in range(8)]
            for e in range(NDOC * 4):
                found = back[half, e // 4, e % 4]
                for i in range(8):
                    accs[i] = jnp.where(each[i] == 4 * e, found, accs[i])
            for i in range(8):
                acc = accs[i] + pltpu.roll(accs[i], 64, 1)
                made.append(acc + pltpu.roll(acc, 32, 1))
        for i in range(8):
            out_ref[block * 8 + i, :, 0:HQ] = made[i][:, 0:HQ]
            out_ref[block * 8 + i, :, HQ:2 * HQ] = made[8 + i][:, HQ:2 * HQ]


def body(
    query_states, token_ids, transform_weight, transform_bias, norm_gain, norm_bias,
    decoder_weight, decoder_bias, candidates, occupancy, doc_blocks,
):
    any_ = pl.BlockSpec(memory_space=pl.ANY)
    vm = pl.BlockSpec(memory_space=pltpu.VMEM)
    dma = pltpu.SemaphoreType.DMA
    weights, back = pl.pallas_call(
        kernel,
        out_shape=(
            jax.ShapeDtypeStruct((QD, VL), BF),
            jax.ShapeDtypeStruct((2, NDOC, 4, 8, 128), F32),
        ),
        in_specs=[any_] * 10,
        out_specs=(any_, any_),
        scratch_shapes=[
            pltpu.VMEM((QD, QLEN, DM), BF),
            pltpu.VMEM((DM, DM), BF),
            pltpu.VMEM((DM, VL), BF),
            pltpu.VMEM((NTL, 128, VL), BF),
            pltpu.VMEM((QLEN, QD), jnp.int32),
            pltpu.VMEM((6, 128), F32),
            pltpu.VMEM((6, 128), F32),
            pltpu.VMEM((6, 128), F32),
            pltpu.VMEM((NB, 128), F32),
            pltpu.VMEM((NTL, NB), jnp.int32),
            pltpu.VMEM((NTL, VL), F32),
            pltpu.VMEM((QD, 128), F32),
            pltpu.VMEM((TOK, DM), BF),
            pltpu.VMEM((QD, VL), BF),
            pltpu.VMEM((2, NDOC, HQ, VL), BF),
            pltpu.VMEM((VL, HL), BF),
            pltpu.VMEM((2, 2, 2, 4, 4, 32, HL), BF),
            pltpu.VMEM((2, 2, 2, 3, 4, 32, HL), BF),
            pltpu.VMEM((2, 2, 2, 4, 32, HL), BF),
            pltpu.VMEM((2, 2, 2, 3, 32, HL), BF),
            pltpu.VMEM((2, NDOC, 4, 8, 128), F32),
            dma((4,)),
            dma((1 + len(BLOCKS),)),
            dma((NB,)),
            dma((6,)),
            dma((3,)),
            dma((4, 4, 2)),
            dma((4, 4, 2)),
            dma((4, 3)),
            dma((4, 3)),
            dma((2, 2, 2, 3)),
            dma((2, 2, 2, 3)),
            dma((2, 2, 2, 3)),
            dma((2, 2, 2, 3)),
            dma((2, NDOC - 1)),
            dma((2, NDOC - 1)),
        ],
        compiler_params=pltpu.CompilerParams(
            collective_id=0, has_side_effects=True, vmem_limit_bytes=60 * 1024 * 1024
        ),
        name="splade",
    )(
        query_states, token_ids.T, transform_weight, transform_bias.reshape(6, 128), norm_gain.reshape(6, 128),
        norm_bias.reshape(6, 128), decoder_weight, decoder_bias.reshape(NB, 128), occupancy, doc_blocks,
    )
    weights, picked = pl.pallas_call(
        pick,
        out_shape=(
            jax.ShapeDtypeStruct((QD, VL), BF),
            jax.ShapeDtypeStruct((CAND, 8, QD), F32),
        ),
        in_specs=[vm, vm, vm],
        out_specs=(vm, vm),
        scratch_shapes=[pltpu.VMEM((2, CAND, 128), jnp.int32)],
        name="pick",
    )(weights, back, candidates.T)
    return weights, picked.transpose(2, 0, 1)


def solution(mesh):
    placed = (
        P("doc", None, None),
        P("doc", None),
        P(),
        P(),
        P(),
        P(),
        P(None, "term"),
        P("term"),
        P("doc", None),
        P("doc", "term"),
        P("doc", "term", None, None),
    )
    return jax.shard_map(
        body,
        mesh=mesh,
        in_specs=placed,
        out_specs=(P("doc", "term"), P("doc", None, "term")),
        check_vma=False,
    )
```

```python
import jax
import jax.numpy as jnp
from jax import lax
from jax.experimental import pallas as pl
from jax.experimental.pallas import tpu as pltpu
from jax.sharding import PartitionSpec as P

MESH = pl.DeviceIdType.MESH
VOCAB = 30522
NDOC = 8
NY = 4
NZ = 4
QD = 64
QLEN = 32
DM = 768
VL = 1920
NB = 15
NTL = 16
CAND = 32
CH = 16
TOK = CH * QLEN
HQ = 32
HL = NDOC * HQ
BLOCKS = ((0, 512), (512, 512), (1024, 512), (1536, 384))
PARTS = ((0, 1024), (1024, 896))
BF = jnp.bfloat16
F32 = jnp.float32


def kernel(
    x_hbm, tok_hbm, tw_hbm, tb_hbm, g_hbm, nb_hbm, dw_hbm, db_hbm, occ_hbm, docs_hbm,
    qw_ref, back,
    xv, twv, dwv, dv, tok_ref, tb_ref, g_ref, nb_ref, db_ref, occ_ref,
    occrow, lens, nrm, qw_v, wall, wt, sbuf, rbuf, s2buf, r2buf, pbuf,
    xsem, wsem, dsem, vsem, osem, ag_s, ag_r, s1_s, s1_r, s2_s, s2_r, rt_s, rt_r,
):
    doc = lax.axis_index("doc")
    term = lax.axis_index("term")
    z = term // NY
    y = lax.rem(term, NY)

    tw_cp = pltpu.make_async_copy(tw_hbm, twv, wsem.at[0])

    def dw_copy(i):
        part = pl.ds(i * (DM // 4), DM // 4)
        return pltpu.make_async_copy(dw_hbm.at[part], dwv.at[part], wsem.at[1])

    def x_copy(c):
        return pltpu.make_async_copy(x_hbm.at[pl.ds(c * CH, CH)], xv.at[pl.ds(c * CH, CH)], xsem.at[c])

    def d_copy(b):
        return pltpu.make_async_copy(docs_hbm.at[:, b], dv.at[:, :, pl.ds(b * 128, 128)], dsem)

    small = [
        pltpu.make_async_copy(a, b, vsem.at[n])
        for n, (a, b) in enumerate((
            (tok_hbm, tok_ref), (tb_hbm, tb_ref), (g_hbm, g_ref), (nb_hbm, nb_ref), (db_hbm, db_ref), (occ_hbm, occ_ref),
        ))
    ]
    tw_cp.start()
    x_copy(0).start()
    for cp in small:
        cp.start()
    for i in range(4):
        dw_copy(i).start()
    for c in range(1, 4):
        x_copy(c).start()
    barrier = pltpu.get_barrier_semaphore()
    for k in range(1, NDOC):
        pl.semaphore_signal(barrier, inc=1, device_id={"doc": lax.rem(doc + k, NDOC)}, device_id_type=MESH)
    for k in range(1, 4):
        pl.semaphore_signal(barrier, inc=1, device_id={"term": z * NY + lax.rem(y + k, NY)}, device_id_type=MESH)
        pl.semaphore_signal(barrier, inc=1, device_id={"term": lax.rem(z + k, NZ) * NY + y}, device_id_type=MESH)

    for cp in small:
        cp.wait()

    live = jnp.where(tok_ref[...] != 0, 1.0, 0.0).astype(BF)
    lens[...] = lax.dot_general(
        live, jnp.ones((QLEN, 128), BF), (((0,), (0,)), ((), ())), preferred_element_type=F32
    )

    def occupancy_rows():
        spread = jnp.where(
            lax.broadcasted_iota(jnp.int32, (NB, VL), 1) // 128 == lax.broadcasted_iota(jnp.int32, (NB, VL), 0), 1.0, 0.0
        ).astype(BF)
        occrow[...] = jnp.dot(occ_ref[...].astype(F32).astype(BF), spread, preferred_element_type=F32)

    def row(ref):
        return jnp.concatenate([ref[i:i + 1, :] for i in range(ref.shape[0])], axis=1)

    tb, gain, nbias, dbias = row(tb_ref), row(g_ref), row(nb_ref), row(db_ref)
    sibling = doc + 1 - 2 * lax.rem(doc, 2)

    def ag_copy(c, k, part):
        half, sub = c // 2, lax.rem(c, 2)
        place = wall.at[half, doc, pl.ds(sub * CH, CH), pl.ds(*PARTS[part])]
        return pltpu.make_async_remote_copy(
            src_ref=place, dst_ref=place, send_sem=ag_s.at[c], recv_sem=ag_r.at[c, 0 if k else 1],
            device_id={"doc": sibling if k == 0 else lax.rem(doc + 2 * k, NDOC)}, device_id_type=MESH,
        )

    def pass_copy(c, k):
        half, sub = c // 2, lax.rem(c, 2)
        place = wall.at[half, lax.rem(doc + NDOC - 2 * k, NDOC), pl.ds(sub * CH, CH)]
        return pltpu.make_async_remote_copy(
            src_ref=place, dst_ref=place, send_sem=ag_s.at[c], recv_sem=ag_r.at[c, 1],
            device_id={"doc": sibling}, device_id_type=MESH,
        )

    def expand(c):
        x_copy(c).wait()
        rows = pl.ds(pl.multiple_of(c * CH, CH), CH)
        h = jnp.dot(xv[rows].reshape(TOK, DM), twv[...], preferred_element_type=F32) + tb
        h = 0.5 * h * (1.0 + lax.erf(h * 0.7071067811865476))
        cen = h - jnp.mean(h, axis=-1, keepdims=True)
        var = jnp.mean(cen * cen, axis=-1, keepdims=True)
        n = cen * lax.rsqrt(var + 1e-6) * gain + nbias
        n3 = n.reshape(CH, QLEN, DM)
        pos = lax.broadcasted_iota(jnp.int32, (CH, QLEN, DM), 1).astype(F32)
        length = jnp.concatenate([lens[rows, :]] * (DM // 128), axis=1)
        n3 = jnp.where(pos < length[:, None, :], n3, n3[:, 0:1, :])
        nrm[...] = n3.reshape(TOK, DM).astype(BF)

    def decode(c):
        half, sub = c // 2, lax.rem(c, 2)
        rows = pl.ds(pl.multiple_of(c * CH, CH), CH)
        srow = pl.ds(pl.multiple_of(sub * CH, CH), CH)
        for c0, COLS in BLOCKS:
            lg = jnp.dot(nrm[...], dwv[:, c0:c0 + COLS], preferred_element_type=F32)
            top = jnp.max(lg.reshape(CH, QLEN, COLS), axis=1) + dbias[:, c0:c0 + COLS]
            w = jnp.log1p(jnp.maximum(top, 0.0))
            col = term * VL + c0 + lax.broadcasted_iota(jnp.int32, (CH, COLS), 1)
            w = jnp.where(col < VOCAB, w, 0.0).astype(BF)
            wall[half, doc, srow, c0:c0 + COLS] = w
            qw_v[rows, c0:c0 + COLS] = w
            for part, (p0, width) in enumerate(PARTS):
                if c0 + COLS == p0 + width:
                    for k in (2, 1, 3, 0):
                        ag_copy(c, k, part).start()

    def ag_rows(c, count, kind):
        rows = wall.at[c // 2, pl.ds(0, count), pl.ds(lax.rem(c, 2) * CH, CH)]
        return pltpu.make_async_remote_copy(
            src_ref=rows, dst_ref=rows, send_sem=ag_s.at[c], recv_sem=ag_r.at[c, kind],
            device_id={"doc": sibling}, device_id_type=MESH,
        )

    def ag_pass(c):
        ag_rows(c, 3, 0).wait_recv()
        for k in (1, 3, 2):
            pass_copy(c, k).start()

    def ag_wait(c):
        ag_rows(c, 4, 1).wait_recv()

    def ag_sent(c):
        ag_rows(c, 7, 0).wait_send()

    def peer_on(first, k):
        py = lax.rem(y + k + 1, NY)
        pz = lax.rem(z + k + 1, NZ)
        return first * py + (1 - first) * pz, first * (z * NY + py) + (1 - first) * (pz * NY + y)

    def s1_copy(half, axis, i, k):
        peer, to = peer_on(1 - axis, k)
        return pltpu.make_async_remote_copy(
            src_ref=sbuf.at[half, axis, i, peer], dst_ref=rbuf.at[half, axis, i, k],
            send_sem=s1_s.at[half, axis, i], recv_sem=s1_r.at[half, axis, i],
            device_id={"term": to}, device_id_type=MESH,
        )

    def s2_copy(half, axis, i, k):
        peer, to = peer_on(axis, k)
        return pltpu.make_async_remote_copy(
            src_ref=s2buf.at[half, axis, i, peer], dst_ref=r2buf.at[half, axis, i, k],
            send_sem=s2_s.at[half, axis, i], recv_sem=s2_r.at[half, axis, i],
            device_id={"term": to}, device_id_type=MESH,
        )

    def s1_all(half, axis, i):
        return pltpu.make_async_remote_copy(
            src_ref=sbuf.at[half, axis, i, pl.ds(0, 3)], dst_ref=rbuf.at[half, axis, i],
            send_sem=s1_s.at[half, axis, i], recv_sem=s1_r.at[half, axis, i],
            device_id={"doc": sibling}, device_id_type=MESH,
        )

    def s2_all(half, axis, i):
        return pltpu.make_async_remote_copy(
            src_ref=s2buf.at[half, axis, i, pl.ds(0, 3)], dst_ref=r2buf.at[half, axis, i],
            send_sem=s2_s.at[half, axis, i], recv_sem=s2_r.at[half, axis, i],
            device_id={"doc": sibling}, device_id_type=MESH,
        )

    def rt_all(half):
        return pltpu.make_async_remote_copy(
            src_ref=pbuf.at[half, pl.ds(0, NDOC - 1)], dst_ref=back.at[half, pl.ds(0, NDOC - 1)],
            send_sem=rt_s.at[half], recv_sem=rt_r.at[half], device_id={"doc": sibling}, device_id_type=MESH,
        )

    def rt_copy(half, k):
        peer = lax.rem(doc + k + 1, NDOC)
        return pltpu.make_async_remote_copy(
            src_ref=pbuf.at[half, peer], dst_ref=back.at[half, doc],
            send_sem=rt_s.at[half], recv_sem=rt_r.at[half], device_id={"doc": peer}, device_id_type=MESH,
        )

    def own_copy(half):
        return pltpu.make_async_copy(pbuf.at[half, doc], back.at[half, doc], osem.at[half])

    def give_back(half):
        for k in range(NDOC - 1):
            rt_copy(half, k).start()
        own_copy(half).start()

    def weights_of(half):
        for c0 in range(0, VL, 128):
            part = wall[half, :, :, c0:c0 + 128].reshape(HL, 128)
            wt[c0:c0 + 128, :] = part.T

    def score(half, i, axis):
        first = pl.multiple_of((2 * i + axis) * 4, 4)

        @pl.when(half == 0)
        def _():
            for t in range(4):
                keep = occrow[pl.ds(first + t, 1), :].astype(BF)
                dv[first + t] = dv[first + t] * keep

        docs = dv[pl.ds(first, 4)].reshape(512, VL)
        r = jnp.dot(docs, wt[...], preferred_element_type=F32).reshape(4, NZ, NY, 8, HL)
        for zz in range(NZ):
            for yy in range(NY):
                part = jnp.concatenate([r[t, zz, yy] for t in range(4)], axis=0).astype(BF)
                sbuf[half, axis, i, yy + axis * (zz - yy), zz + axis * (yy - zz)] = part
        for k in (1, 0, 2):
            s1_copy(half, axis, i, k).start()

    def reduce1(half, i, axis):
        s1_all(half, axis, i).wait_recv()
        tot = sbuf[half, axis, i, y + axis * (z - y)].astype(F32)
        for k in range(3):
            tot = tot + rbuf[half, axis, i, k].astype(F32)
        s2buf[half, axis, i] = tot.astype(BF)
        for k in (1, 0, 2):
            s2_copy(half, axis, i, k).start()
        s1_all(half, axis, i).wait_send()

    def reduce2(half, i, axis):
        lane_group = lax.broadcasted_iota(jnp.int32, (8, 128), 1) // HQ
        s2_all(half, axis, i).wait_recv()
        tot = s2buf[half, axis, i, z + axis * (y - z)].astype(F32)
        for k in range(3):
            tot = tot + r2buf[half, axis, i, k].astype(F32)
        for j in range(NDOC):
            made = jnp.zeros((8, 128), F32)
            for t in range(4):
                piece = tot[t * 8:(t + 1) * 8, (j // 4) * 128:(j // 4 + 1) * 128]
                turn = ((t - j % 4) * HQ) % 128
                if turn:
                    piece = pltpu.roll(piece, turn, 1)
                made = jnp.where(lane_group == t, piece, made)
            pbuf[half, j, 2 * i + axis] = made

    tw_cp.wait()

    @pl.loop(0, 4)
    def _(c):
        expand(c)

        @pl.when(c == 0)
        def _():
            pltpu.make_async_copy(dwv, dwv, wsem.at[1]).wait()
            pl.semaphore_wait(barrier, NDOC - 1 + 6)
            for b in range(NB):
                d_copy(b).start()

        @pl.when(c >= 2)
        def _():
            ag_pass(c - 2)

        decode(c)

    qw_cp = pltpu.make_async_copy(qw_v, qw_ref, osem.at[2])
    qw_cp.start()
    occupancy_rows()
    pltpu.make_async_copy(dv, dv, dsem).wait()

    @pl.loop(0, 2)
    def _(half):
        @pl.when(half == 1)
        def _():
            ag_pass(3)

        ag_wait(2 * half)
        ag_wait(2 * half + 1)
        weights_of(half)

        @pl.loop(0, 4)
        def _(n):
            score(half, n // 2, lax.rem(n, 2))

            @pl.when((half == 0) & (n == 1))
            def _():
                ag_pass(2)

    @pl.loop(0, 8)
    def _(n):
        reduce1(n // 4, lax.rem(n // 2, 2), lax.rem(n, 2))

    @pl.loop(0, 4)
    def _(c):
        ag_sent(c)

    @pl.loop(0, 2)
    def _(half):
        @pl.loop(0, 4)
        def _(n):
            reduce2(half, n // 2, lax.rem(n, 2))

        give_back(half)

    @pl.loop(0, 8)
    def _(n):
        s2_all(n // 4, lax.rem(n, 2), lax.rem(n // 2, 2)).wait_send()

    qw_cp.wait()
    for half in range(2):
        own_copy(half).wait()
        rt_all(half).wait()


def pick(qw_ref, back, cand_ref, qw_out, out_ref, want):
    qw_out[...] = qw_ref[...]
    part = lax.broadcasted_iota(jnp.int32, (CAND, 128), 1) // HQ
    for half in range(2):
        mine = cand_ref[:, half * HQ:(half + 1) * HQ]
        want[half] = jnp.concatenate([mine] * 4, axis=1) - part

    @pl.loop(0, CAND // 8)
    def _(block):
        made = []
        for half in range(2):
            rows = want[half, pl.ds(pl.multiple_of(block * 8, 8), 8), :]
            each = [jnp.broadcast_to(rows[i:i + 1, :], (8, 128)) for i in range(8)]
            accs = [jnp.zeros((8, 128), F32) for _ in range(8)]
            for e in range(NDOC * 4):
                found = back[half, e // 4, e % 4]
                for i in range(8):
                    accs[i] = jnp.where(each[i] == 4 * e, found, accs[i])
            for i in range(8):
                acc = accs[i] + pltpu.roll(accs[i], 64, 1)
                made.append(acc + pltpu.roll(acc, 32, 1))
        for i in range(8):
            out_ref[block * 8 + i, :, 0:HQ] = made[i][:, 0:HQ]
            out_ref[block * 8 + i, :, HQ:2 * HQ] = made[8 + i][:, HQ:2 * HQ]


def body(
    query_states, token_ids, transform_weight, transform_bias, norm_gain, norm_bias,
    decoder_weight, decoder_bias, candidates, occupancy, doc_blocks,
):
    any_ = pl.BlockSpec(memory_space=pl.ANY)
    vm = pl.BlockSpec(memory_space=pltpu.VMEM)
    dma = pltpu.SemaphoreType.DMA
    weights, back = pl.pallas_call(
        kernel,
        out_shape=(
            jax.ShapeDtypeStruct((QD, VL), BF),
            jax.ShapeDtypeStruct((2, NDOC, 4, 8, 128), F32),
        ),
        in_specs=[any_] * 10,
        out_specs=(any_, any_),
        scratch_shapes=[
            pltpu.VMEM((QD, QLEN, DM), BF),
            pltpu.VMEM((DM, DM), BF),
            pltpu.VMEM((DM, VL), BF),
            pltpu.VMEM((NTL, 128, VL), BF),
            pltpu.VMEM((QLEN, QD), jnp.int32),
            pltpu.VMEM((6, 128), F32),
            pltpu.VMEM((6, 128), F32),
            pltpu.VMEM((6, 128), F32),
            pltpu.VMEM((NB, 128), F32),
            pltpu.VMEM((NTL, NB), jnp.int32),
            pltpu.VMEM((NTL, VL), F32),
            pltpu.VMEM((QD, 128), F32),
            pltpu.VMEM((TOK, DM), BF),
            pltpu.VMEM((QD, VL), BF),
            pltpu.VMEM((2, NDOC, HQ, VL), BF),
            pltpu.VMEM((VL, HL), BF),
            pltpu.VMEM((2, 2, 2, 4, 4, 32, HL), BF),
            pltpu.VMEM((2, 2, 2, 3, 4, 32, HL), BF),
            pltpu.VMEM((2, 2, 2, 4, 32, HL), BF),
            pltpu.VMEM((2, 2, 2, 3, 32, HL), BF),
            pltpu.VMEM((2, NDOC, 4, 8, 128), F32),
            dma((4,)),
            dma((2,)),
            dma(()),
            dma((6,)),
            dma((3,)),
            dma((4,)),
            dma((4, 2)),
            dma((2, 2, 2)),
            dma((2, 2, 2)),
            dma((2, 2, 2)),
            dma((2, 2, 2)),
            dma((2,)),
            dma((2,)),
        ],
        compiler_params=pltpu.CompilerParams(
            collective_id=0, has_side_effects=True, vmem_limit_bytes=60 * 1024 * 1024
        ),
        name="splade",
    )(
        query_states, token_ids.T, transform_weight, transform_bias.reshape(6, 128), norm_gain.reshape(6, 128),
        norm_bias.reshape(6, 128), decoder_weight, decoder_bias.reshape(NB, 128), occupancy, doc_blocks,
    )
    weights, picked = pl.pallas_call(
        pick,
        out_shape=(
            jax.ShapeDtypeStruct((QD, VL), BF),
            jax.ShapeDtypeStruct((CAND, 8, QD), F32),
        ),
        in_specs=[vm, vm, vm],
        out_specs=(vm, vm),
        scratch_shapes=[pltpu.VMEM((2, CAND, 128), jnp.int32)],
        name="pick",
    )(weights, back, candidates.T)
    return weights, picked.transpose(2, 0, 1)


def solution(mesh):
    placed = (
        P("doc", None, None),
        P("doc", None),
        P(),
        P(),
        P(),
        P(),
        P(None, "term"),
        P("term"),
        P("doc", None),
        P("doc", "term"),
        P("doc", "term", None, None),
    )
    return jax.shard_map(
        body,
        mesh=mesh,
        in_specs=placed,
        out_specs=(P("doc", "term"), P("doc", None, "term")),
        check_vma=False,
    )
```

```python
import jax
import jax.numpy as jnp
from jax import lax
from jax.experimental import pallas as pl
from jax.experimental.pallas import tpu as pltpu
from jax.sharding import PartitionSpec as P

MESH = pl.DeviceIdType.MESH
VOCAB = 30522
NDOC = 8
NY = 4
NZ = 4
QD = 64
QLEN = 32
DM = 768
VL = 1920
NB = 15
NTL = 16
CAND = 32
CH = 16
TOK = CH * QLEN
HQ = 32
HL = NDOC * HQ
BLOCKS = ((0, 512), (512, 512), (1024, 512), (1536, 384))
PARTS = ((0, 1920),)
BF = jnp.bfloat16
F32 = jnp.float32


def kernel(
    x_hbm, tok_hbm, tw_hbm, tb_hbm, g_hbm, nb_hbm, dw_hbm, db_hbm, occ_hbm, docs_hbm,
    qw_ref, back,
    xv, twv, dwv, dv, tok_ref, tb_ref, g_ref, nb_ref, db_ref, occ_ref,
    occrow, lens, nrm, qw_v, wall, wt, sbuf, rbuf, s2buf, r2buf, pbuf,
    xsem, wsem, dsem, vsem, osem, ag_s, ag_r, s1_s, s1_r, s2_s, s2_r, rt_s, rt_r,
):
    doc = lax.axis_index("doc")
    term = lax.axis_index("term")
    z = term // NY
    y = lax.rem(term, NY)

    tw_cp = pltpu.make_async_copy(tw_hbm, twv, wsem.at[0])

    def dw_copy(i):
        part = pl.ds(i * (DM // 4), DM // 4)
        return pltpu.make_async_copy(dw_hbm.at[part], dwv.at[part], wsem.at[1])

    def x_copy(c):
        return pltpu.make_async_copy(x_hbm.at[pl.ds(c * CH, CH)], xv.at[pl.ds(c * CH, CH)], xsem.at[c])

    def d_copy(b):
        return pltpu.make_async_copy(docs_hbm.at[:, b], dv.at[:, :, pl.ds(b * 128, 128)], dsem)

    small = [
        pltpu.make_async_copy(a, b, vsem.at[n])
        for n, (a, b) in enumerate((
            (tok_hbm, tok_ref), (tb_hbm, tb_ref), (g_hbm, g_ref), (nb_hbm, nb_ref), (db_hbm, db_ref), (occ_hbm, occ_ref),
        ))
    ]
    tw_cp.start()
    x_copy(0).start()
    for cp in small:
        cp.start()
    for i in range(4):
        dw_copy(i).start()
    for c in range(1, 4):
        x_copy(c).start()
    barrier = pltpu.get_barrier_semaphore()
    for k in range(1, NDOC):
        pl.semaphore_signal(barrier, inc=1, device_id={"doc": lax.rem(doc + k, NDOC)}, device_id_type=MESH)
    for k in range(1, 4):
        pl.semaphore_signal(barrier, inc=1, device_id={"term": z * NY + lax.rem(y + k, NY)}, device_id_type=MESH)
        pl.semaphore_signal(barrier, inc=1, device_id={"term": lax.rem(z + k, NZ) * NY + y}, device_id_type=MESH)

    for cp in small:
        cp.wait()

    live = jnp.where(tok_ref[...] != 0, 1.0, 0.0).astype(BF)
    lens[...] = lax.dot_general(
        live, jnp.ones((QLEN, 128), BF), (((0,), (0,)), ((), ())), preferred_element_type=F32
    )

    def occupancy_rows():
        spread = jnp.where(
            lax.broadcasted_iota(jnp.int32, (NB, VL), 1) // 128 == lax.broadcasted_iota(jnp.int32, (NB, VL), 0), 1.0, 0.0
        ).astype(BF)
        occrow[...] = jnp.dot(occ_ref[...].astype(F32).astype(BF), spread, preferred_element_type=F32)

    def row(ref):
        return jnp.concatenate([ref[i:i + 1, :] for i in range(ref.shape[0])], axis=1)

    tb, gain, nbias, dbias = row(tb_ref), row(g_ref), row(nb_ref), row(db_ref)
    sibling = doc + 1 - 2 * lax.rem(doc, 2)

    def ag_copy(c, k, part):
        half, sub = c // 2, lax.rem(c, 2)
        place = wall.at[half, doc, pl.ds(sub * CH, CH), pl.ds(*PARTS[part])]
        return pltpu.make_async_remote_copy(
            src_ref=place, dst_ref=place, send_sem=ag_s.at[c], recv_sem=ag_r.at[c, 0 if k else 1],
            device_id={"doc": sibling if k == 0 else lax.rem(doc + 2 * k, NDOC)}, device_id_type=MESH,
        )

    def pass_copy(c, k):
        half, sub = c // 2, lax.rem(c, 2)
        place = wall.at[half, lax.rem(doc + NDOC - 2 * k, NDOC), pl.ds(sub * CH, CH)]
        return pltpu.make_async_remote_copy(
            src_ref=place, dst_ref=place, send_sem=ag_s.at[c], recv_sem=ag_r.at[c, 1],
            device_id={"doc": sibling}, device_id_type=MESH,
        )

    def expand(c):
        x_copy(c).wait()
        rows = pl.ds(pl.multiple_of(c * CH, CH), CH)
        h = jnp.dot(xv[rows].reshape(TOK, DM), twv[...], preferred_element_type=F32) + tb
        h = 0.5 * h * (1.0 + lax.erf(h * 0.7071067811865476))
        cen = h - jnp.mean(h, axis=-1, keepdims=True)
        var = jnp.mean(cen * cen, axis=-1, keepdims=True)
        n = cen * lax.rsqrt(var + 1e-6) * gain + nbias
        n3 = n.reshape(CH, QLEN, DM)
        pos = lax.broadcasted_iota(jnp.int32, (CH, QLEN, DM), 1).astype(F32)
        length = jnp.concatenate([lens[rows, :]] * (DM // 128), axis=1)
        n3 = jnp.where(pos < length[:, None, :], n3, n3[:, 0:1, :])
        nrm[...] = n3.reshape(TOK, DM).astype(BF)

    def decode(c):
        half, sub = c // 2, lax.rem(c, 2)
        rows = pl.ds(pl.multiple_of(c * CH, CH), CH)
        srow = pl.ds(pl.multiple_of(sub * CH, CH), CH)
        for c0, COLS in BLOCKS:
            lg = jnp.dot(nrm[...], dwv[:, c0:c0 + COLS], preferred_element_type=F32)
            top = jnp.max(lg.reshape(CH, QLEN, COLS), axis=1) + dbias[:, c0:c0 + COLS]
            w = jnp.log1p(jnp.maximum(top, 0.0))
            col = term * VL + c0 + lax.broadcasted_iota(jnp.int32, (CH, COLS), 1)
            w = jnp.where(col < VOCAB, w, 0.0).astype(BF)
            wall[half, doc, srow, c0:c0 + COLS] = w
            qw_v[rows, c0:c0 + COLS] = w
            for part, (p0, width) in enumerate(PARTS):
                if c0 + COLS == p0 + width:
                    for k in (2, 1, 3, 0):
                        ag_copy(c, k, part).start()

    def ag_rows(c, count, kind):
        rows = wall.at[c // 2, pl.ds(0, count), pl.ds(lax.rem(c, 2) * CH, CH)]
        return pltpu.make_async_remote_copy(
            src_ref=rows, dst_ref=rows, send_sem=ag_s.at[c], recv_sem=ag_r.at[c, kind],
            device_id={"doc": sibling}, device_id_type=MESH,
        )

    def ag_pass(c):
        ag_rows(c, 3, 0).wait_recv()
        for k in (1, 3, 2):
            pass_copy(c, k).start()

    def ag_wait(c):
        ag_rows(c, 4, 1).wait_recv()

    def ag_sent(c):
        ag_rows(c, 7, 0).wait_send()

    def peer_on(first, k):
        py = lax.rem(y + k + 1, NY)
        pz = lax.rem(z + k + 1, NZ)
        return first * py + (1 - first) * pz, first * (z * NY + py) + (1 - first) * (pz * NY + y)

    def s1_copy(half, axis, i, k):
        peer, to = peer_on(1 - axis, k)
        return pltpu.make_async_remote_copy(
            src_ref=sbuf.at[half, axis, i, peer], dst_ref=rbuf.at[half, axis, i, k],
            send_sem=s1_s.at[half, axis, i], recv_sem=s1_r.at[half, axis, i],
            device_id={"term": to}, device_id_type=MESH,
        )

    def s2_copy(half, axis, i, k):
        peer, to = peer_on(axis, k)
        return pltpu.make_async_remote_copy(
            src_ref=s2buf.at[half, axis, i, peer], dst_ref=r2buf.at[half, axis, i, k],
            send_sem=s2_s.at[half, axis, i], recv_sem=s2_r.at[half, axis, i],
            device_id={"term": to}, device_id_type=MESH,
        )

    def s1_all(half, axis, i):
        return pltpu.make_async_remote_copy(
            src_ref=sbuf.at[half, axis, i, pl.ds(0, 3)], dst_ref=rbuf.at[half, axis, i],
            send_sem=s1_s.at[half, axis, i], recv_sem=s1_r.at[half, axis, i],
            device_id={"doc": sibling}, device_id_type=MESH,
        )

    def s2_all(half, axis, i):
        return pltpu.make_async_remote_copy(
            src_ref=s2buf.at[half, axis, i, pl.ds(0, 3)], dst_ref=r2buf.at[half, axis, i],
            send_sem=s2_s.at[half, axis, i], recv_sem=s2_r.at[half, axis, i],
            device_id={"doc": sibling}, device_id_type=MESH,
        )

    def rt_all(half):
        return pltpu.make_async_remote_copy(
            src_ref=pbuf.at[half, pl.ds(0, NDOC - 1)], dst_ref=back.at[half, pl.ds(0, NDOC - 1)],
            send_sem=rt_s.at[half], recv_sem=rt_r.at[half], device_id={"doc": sibling}, device_id_type=MESH,
        )

    def rt_copy(half, k):
        peer = lax.rem(doc + k + 1, NDOC)
        return pltpu.make_async_remote_copy(
            src_ref=pbuf.at[half, peer], dst_ref=back.at[half, doc],
            send_sem=rt_s.at[half], recv_sem=rt_r.at[half], device_id={"doc": peer}, device_id_type=MESH,
        )

    def own_copy(half):
        return pltpu.make_async_copy(pbuf.at[half, doc], back.at[half, doc], osem.at[half])

    def give_back(half):
        for k in range(NDOC - 1):
            rt_copy(half, k).start()
        own_copy(half).start()

    def weights_of(half):
        for c0 in range(0, VL, 128):
            part = wall[half, :, :, c0:c0 + 128].reshape(HL, 128)
            wt[c0:c0 + 128, :] = part.T

    def score(half, i, axis):
        first = pl.multiple_of((2 * i + axis) * 4, 4)

        @pl.when(half == 0)
        def _():
            for t in range(4):
                keep = occrow[pl.ds(first + t, 1), :].astype(BF)
                dv[first + t] = dv[first + t] * keep

        docs = dv[pl.ds(first, 4)].reshape(512, VL)
        r = jnp.dot(docs, wt[...], preferred_element_type=F32).reshape(4, NZ, NY, 8, HL)
        for zz in range(NZ):
            for yy in range(NY):
                part = jnp.concatenate([r[t, zz, yy] for t in range(4)], axis=0).astype(BF)
                sbuf[half, axis, i, yy + axis * (zz - yy), zz + axis * (yy - zz)] = part
        for k in (1, 0, 2):
            s1_copy(half, axis, i, k).start()

    def reduce1(half, i, axis):
        s1_all(half, axis, i).wait_recv()
        tot = sbuf[half, axis, i, y + axis * (z - y)].astype(F32)
        for k in range(3):
            tot = tot + rbuf[half, axis, i, k].astype(F32)
        s2buf[half, axis, i] = tot.astype(BF)
        for k in (1, 0, 2):
            s2_copy(half, axis, i, k).start()
        s1_all(half, axis, i).wait_send()

    def reduce2(half, i, axis):
        lane_group = lax.broadcasted_iota(jnp.int32, (8, 128), 1) // HQ
        s2_all(half, axis, i).wait_recv()
        tot = s2buf[half, axis, i, z + axis * (y - z)].astype(F32)
        for k in range(3):
            tot = tot + r2buf[half, axis, i, k].astype(F32)
        for j in range(NDOC):
            made = jnp.zeros((8, 128), F32)
            for t in range(4):
                piece = tot[t * 8:(t + 1) * 8, (j // 4) * 128:(j // 4 + 1) * 128]
                turn = ((t - j % 4) * HQ) % 128
                if turn:
                    piece = pltpu.roll(piece, turn, 1)
                made = jnp.where(lane_group == t, piece, made)
            pbuf[half, j, 2 * i + axis] = made

    tw_cp.wait()

    @pl.loop(0, 4)
    def _(c):
        expand(c)

        @pl.when(c == 0)
        def _():
            pltpu.make_async_copy(dwv, dwv, wsem.at[1]).wait()
            pl.semaphore_wait(barrier, NDOC - 1 + 6)
            for b in range(NB):
                d_copy(b).start()

        @pl.when(c >= 2)
        def _():
            ag_pass(c - 2)

        decode(c)

    qw_cp = pltpu.make_async_copy(qw_v, qw_ref, osem.at[2])
    qw_cp.start()
    occupancy_rows()
    pltpu.make_async_copy(dv, dv, dsem).wait()

    @pl.loop(0, 2)
    def _(half):
        @pl.when(half == 1)
        def _():
            ag_pass(3)

        ag_wait(2 * half)
        ag_wait(2 * half + 1)
        weights_of(half)

        @pl.loop(0, 4)
        def _(n):
            score(half, n // 2, lax.rem(n, 2))

            @pl.when((half == 0) & (n == 1))
            def _():
                ag_pass(2)

    @pl.loop(0, 8)
    def _(n):
        reduce1(n // 4, lax.rem(n // 2, 2), lax.rem(n, 2))

    @pl.loop(0, 4)
    def _(c):
        ag_sent(c)

    @pl.loop(0, 2)
    def _(half):
        @pl.loop(0, 4)
        def _(n):
            reduce2(half, n // 2, lax.rem(n, 2))

        give_back(half)

    @pl.loop(0, 8)
    def _(n):
        s2_all(n // 4, lax.rem(n, 2), lax.rem(n // 2, 2)).wait_send()

    qw_cp.wait()
    for half in range(2):
        own_copy(half).wait()
        rt_all(half).wait()


def pick(qw_ref, back, cand_ref, qw_out, out_ref, want):
    qw_out[...] = qw_ref[...]
    part = lax.broadcasted_iota(jnp.int32, (CAND, 128), 1) // HQ
    for half in range(2):
        mine = cand_ref[:, half * HQ:(half + 1) * HQ]
        want[half] = jnp.concatenate([mine] * 4, axis=1) - part

    @pl.loop(0, CAND // 8)
    def _(block):
        made = []
        for half in range(2):
            rows = want[half, pl.ds(pl.multiple_of(block * 8, 8), 8), :]
            each = [jnp.broadcast_to(rows[i:i + 1, :], (8, 128)) for i in range(8)]
            accs = [jnp.zeros((8, 128), F32) for _ in range(8)]
            for e in range(NDOC * 4):
                found = back[half, e // 4, e % 4]
                for i in range(8):
                    accs[i] = jnp.where(each[i] == 4 * e, found, accs[i])
            for i in range(8):
                acc = accs[i] + pltpu.roll(accs[i], 64, 1)
                made.append(acc + pltpu.roll(acc, 32, 1))
        for i in range(8):
            out_ref[block * 8 + i, :, 0:HQ] = made[i][:, 0:HQ]
            out_ref[block * 8 + i, :, HQ:2 * HQ] = made[8 + i][:, HQ:2 * HQ]


def body(
    query_states, token_ids, transform_weight, transform_bias, norm_gain, norm_bias,
    decoder_weight, decoder_bias, candidates, occupancy, doc_blocks,
):
    any_ = pl.BlockSpec(memory_space=pl.ANY)
    vm = pl.BlockSpec(memory_space=pltpu.VMEM)
    dma = pltpu.SemaphoreType.DMA
    weights, back = pl.pallas_call(
        kernel,
        out_shape=(
            jax.ShapeDtypeStruct((QD, VL), BF),
            jax.ShapeDtypeStruct((2, NDOC, 4, 8, 128), F32),
        ),
        in_specs=[any_] * 10,
        out_specs=(any_, any_),
        scratch_shapes=[
            pltpu.VMEM((QD, QLEN, DM), BF),
            pltpu.VMEM((DM, DM), BF),
            pltpu.VMEM((DM, VL), BF),
            pltpu.VMEM((NTL, 128, VL), BF),
            pltpu.VMEM((QLEN, QD), jnp.int32),
            pltpu.VMEM((6, 128), F32),
            pltpu.VMEM((6, 128), F32),
            pltpu.VMEM((6, 128), F32),
            pltpu.VMEM((NB, 128), F32),
            pltpu.VMEM((NTL, NB), jnp.int32),
            pltpu.VMEM((NTL, VL), F32),
            pltpu.VMEM((QD, 128), F32),
            pltpu.VMEM((TOK, DM), BF),
            pltpu.VMEM((QD, VL), BF),
            pltpu.VMEM((2, NDOC, HQ, VL), BF),
            pltpu.VMEM((VL, HL), BF),
            pltpu.VMEM((2, 2, 2, 4, 4, 32, HL), BF),
            pltpu.VMEM((2, 2, 2, 3, 4, 32, HL), BF),
            pltpu.VMEM((2, 2, 2, 4, 32, HL), BF),
            pltpu.VMEM((2, 2, 2, 3, 32, HL), BF),
            pltpu.VMEM((2, NDOC, 4, 8, 128), F32),
            dma((4,)),
            dma((2,)),
            dma(()),
            dma((6,)),
            dma((3,)),
            dma((4,)),
            dma((4, 2)),
            dma((2, 2, 2)),
            dma((2, 2, 2)),
            dma((2, 2, 2)),
            dma((2, 2, 2)),
            dma((2,)),
            dma((2,)),
        ],
        compiler_params=pltpu.CompilerParams(
            collective_id=0, has_side_effects=True, vmem_limit_bytes=60 * 1024 * 1024
        ),
        name="splade",
    )(
        query_states, token_ids.T, transform_weight, transform_bias.reshape(6, 128), norm_gain.reshape(6, 128),
        norm_bias.reshape(6, 128), decoder_weight, decoder_bias.reshape(NB, 128), occupancy, doc_blocks,
    )
    weights, picked = pl.pallas_call(
        pick,
        out_shape=(
            jax.ShapeDtypeStruct((QD, VL), BF),
            jax.ShapeDtypeStruct((CAND, 8, QD), F32),
        ),
        in_specs=[vm, vm, vm],
        out_specs=(vm, vm),
        scratch_shapes=[pltpu.VMEM((2, CAND, 128), jnp.int32)],
        name="pick",
    )(weights, back, candidates.T)
    return weights, picked.transpose(2, 0, 1)


def solution(mesh):
    placed = (
        P("doc", None, None),
        P("doc", None),
        P(),
        P(),
        P(),
        P(),
        P(None, "term"),
        P("term"),
        P("doc", None),
        P("doc", "term"),
        P("doc", "term", None, None),
    )
    return jax.shard_map(
        body,
        mesh=mesh,
        in_specs=placed,
        out_specs=(P("doc", "term"), P("doc", None, "term")),
        check_vma=False,
    )
```

```python
import jax
import jax.numpy as jnp
from jax import lax
from jax.experimental import pallas as pl
from jax.experimental.pallas import tpu as pltpu
from jax.sharding import PartitionSpec as P

MESH = pl.DeviceIdType.MESH
VOCAB = 30522
NDOC = 8
NY = 4
NZ = 4
QD = 64
QLEN = 32
DM = 768
VL = 1920
NB = 15
NTL = 16
CAND = 32
CH = 16
TOK = CH * QLEN
HQ = 32
HL = NDOC * HQ
BLOCKS = ((0, 512), (512, 512), (1024, 512), (1536, 384))
PARTS = ((0, 1920),)
BF = jnp.bfloat16
F32 = jnp.float32


def kernel(
    x_hbm, tok_hbm, tw_hbm, tb_hbm, g_hbm, nb_hbm, dw_hbm, db_hbm, occ_hbm, docs_hbm,
    qw_ref, back,
    xv, twv, dwv, dv, tok_ref, tb_ref, g_ref, nb_ref, db_ref, occ_ref,
    occrow, lens, nrm, qw_v, wall, wt, sbuf, rbuf, s2buf, r2buf, pbuf,
    xsem, wsem, dsem, vsem, osem, ag_s, ag_r, s1_s, s1_r, s2_s, s2_r, rt_s, rt_r,
):
    doc = lax.axis_index("doc")
    term = lax.axis_index("term")
    z = term // NY
    y = lax.rem(term, NY)

    tw_cp = pltpu.make_async_copy(tw_hbm, twv, wsem.at[0])

    def dw_copy(i):
        part = pl.ds(i * (DM // 4), DM // 4)
        return pltpu.make_async_copy(dw_hbm.at[part], dwv.at[part], wsem.at[1])

    def x_copy(c):
        return pltpu.make_async_copy(x_hbm.at[pl.ds(c * CH, CH)], xv.at[pl.ds(c * CH, CH)], xsem.at[c])

    def d_copy(b):
        return pltpu.make_async_copy(docs_hbm.at[:, b], dv.at[:, :, pl.ds(b * 128, 128)], dsem)

    small = [
        pltpu.make_async_copy(a, b, vsem.at[n])
        for n, (a, b) in enumerate((
            (tok_hbm, tok_ref), (tb_hbm, tb_ref), (g_hbm, g_ref), (nb_hbm, nb_ref), (db_hbm, db_ref), (occ_hbm, occ_ref),
        ))
    ]
    tw_cp.start()
    x_copy(0).start()
    for cp in small:
        cp.start()
    for i in range(4):
        dw_copy(i).start()
    for c in range(1, 4):
        x_copy(c).start()
    barrier = pltpu.get_barrier_semaphore()
    for k in range(1, NDOC):
        pl.semaphore_signal(barrier, inc=1, device_id={"doc": lax.rem(doc + k, NDOC)}, device_id_type=MESH)
    for k in range(1, 4):
        pl.semaphore_signal(barrier, inc=1, device_id={"term": z * NY + lax.rem(y + k, NY)}, device_id_type=MESH)
        pl.semaphore_signal(barrier, inc=1, device_id={"term": lax.rem(z + k, NZ) * NY + y}, device_id_type=MESH)

    for cp in small:
        cp.wait()

    live = jnp.where(tok_ref[...] != 0, 1.0, 0.0).astype(BF)
    lens[...] = lax.dot_general(
        live, jnp.ones((QLEN, 128), BF), (((0,), (0,)), ((), ())), preferred_element_type=F32
    )

    def occupancy_rows():
        spread = jnp.where(
            lax.broadcasted_iota(jnp.int32, (NB, VL), 1) // 128 == lax.broadcasted_iota(jnp.int32, (NB, VL), 0), 1.0, 0.0
        ).astype(BF)
        occrow[...] = jnp.dot(occ_ref[...].astype(F32).astype(BF), spread, preferred_element_type=F32)

    def row(ref):
        return jnp.concatenate([ref[i:i + 1, :] for i in range(ref.shape[0])], axis=1)

    tb, gain, nbias, dbias = row(tb_ref), row(g_ref), row(nb_ref), row(db_ref)
    sibling = doc + 1 - 2 * lax.rem(doc, 2)

    def ag_copy(c, k, part):
        half, sub = c // 2, lax.rem(c, 2)
        place = wall.at[half, doc, pl.ds(sub * CH, CH), pl.ds(*PARTS[part])]
        return pltpu.make_async_remote_copy(
            src_ref=place, dst_ref=place, send_sem=ag_s.at[c], recv_sem=ag_r.at[c, 0 if k else 1],
            device_id={"doc": sibling if k == 0 else lax.rem(doc + 2 * k, NDOC)}, device_id_type=MESH,
        )

    def pass_copy(c, k):
        half, sub = c // 2, lax.rem(c, 2)
        place = wall.at[half, lax.rem(doc + NDOC - 2 * k, NDOC), pl.ds(sub * CH, CH)]
        return pltpu.make_async_remote_copy(
            src_ref=place, dst_ref=place, send_sem=ag_s.at[c], recv_sem=ag_r.at[c, 1],
            device_id={"doc": sibling}, device_id_type=MESH,
        )

    def expand(c):
        x_copy(c).wait()
        rows = pl.ds(pl.multiple_of(c * CH, CH), CH)
        h = jnp.dot(xv[rows].reshape(TOK, DM), twv[...], preferred_element_type=F32) + tb
        h = 0.5 * h * (1.0 + lax.erf(h * 0.7071067811865476))
        cen = h - jnp.mean(h, axis=-1, keepdims=True)
        var = jnp.mean(cen * cen, axis=-1, keepdims=True)
        n = cen * lax.rsqrt(var + 1e-6) * gain + nbias
        n3 = n.reshape(CH, QLEN, DM)
        pos = lax.broadcasted_iota(jnp.int32, (CH, QLEN, DM), 1).astype(F32)
        length = jnp.concatenate([lens[rows, :]] * (DM // 128), axis=1)
        n3 = jnp.where(pos < length[:, None, :], n3, n3[:, 0:1, :])
        nrm[...] = n3.reshape(TOK, DM).astype(BF)

    def decode(c):
        half, sub = c // 2, lax.rem(c, 2)
        rows = pl.ds(pl.multiple_of(c * CH, CH), CH)
        srow = pl.ds(pl.multiple_of(sub * CH, CH), CH)
        for c0, COLS in BLOCKS:
            lg = jnp.dot(nrm[...], dwv[:, c0:c0 + COLS], preferred_element_type=F32)
            top = jnp.max(lg.reshape(CH, QLEN, COLS), axis=1) + dbias[:, c0:c0 + COLS]
            w = jnp.log1p(jnp.maximum(top, 0.0))
            col = term * VL + c0 + lax.broadcasted_iota(jnp.int32, (CH, COLS), 1)
            w = jnp.where(col < VOCAB, w, 0.0).astype(BF)
            wall[half, doc, srow, c0:c0 + COLS] = w
            qw_v[rows, c0:c0 + COLS] = w
            for part, (p0, width) in enumerate(PARTS):
                if c0 + COLS == p0 + width:
                    for k in (2, 1, 3, 0):
                        ag_copy(c, k, part).start()

    def ag_rows(c, count, kind):
        rows = wall.at[c // 2, pl.ds(0, count), pl.ds(lax.rem(c, 2) * CH, CH)]
        return pltpu.make_async_remote_copy(
            src_ref=rows, dst_ref=rows, send_sem=ag_s.at[c], recv_sem=ag_r.at[c, kind],
            device_id={"doc": sibling}, device_id_type=MESH,
        )

    def ag_pass(c):
        ag_rows(c, 3, 0).wait_recv()
        for k in (1, 3, 2):
            pass_copy(c, k).start()

    def ag_wait(c):
        ag_rows(c, 4, 1).wait_recv()

    def ag_sent(c):
        ag_rows(c, 7, 0).wait_send()

    def peer_on(first, k):
        py = lax.rem(y + k + 1, NY)
        pz = lax.rem(z + k + 1, NZ)
        return first * py + (1 - first) * pz, first * (z * NY + py) + (1 - first) * (pz * NY + y)

    def s1_copy(half, axis, i, k):
        peer, to = peer_on(1 - axis, k)
        return pltpu.make_async_remote_copy(
            src_ref=sbuf.at[half, axis, i, peer], dst_ref=rbuf.at[half, axis, i, k],
            send_sem=s1_s.at[half, axis, i], recv_sem=s1_r.at[half, axis, i],
            device_id={"term": to}, device_id_type=MESH,
        )

    def s2_copy(half, axis, i, k):
        peer, to = peer_on(axis, k)
        return pltpu.make_async_remote_copy(
            src_ref=s2buf.at[half, axis, i, peer], dst_ref=r2buf.at[half, axis, i, k],
            send_sem=s2_s.at[half, axis, i], recv_sem=s2_r.at[half, axis, i],
            device_id={"term": to}, device_id_type=MESH,
        )

    def s1_all(half, axis, i):
        return pltpu.make_async_remote_copy(
            src_ref=sbuf.at[half, axis, i, pl.ds(0, 3)], dst_ref=rbuf.at[half, axis, i],
            send_sem=s1_s.at[half, axis, i], recv_sem=s1_r.at[half, axis, i],
            device_id={"doc": sibling}, device_id_type=MESH,
        )

    def s2_all(half, axis, i):
        return pltpu.make_async_remote_copy(
            src_ref=s2buf.at[half, axis, i, pl.ds(0, 3)], dst_ref=r2buf.at[half, axis, i],
            send_sem=s2_s.at[half, axis, i], recv_sem=s2_r.at[half, axis, i],
            device_id={"doc": sibling}, device_id_type=MESH,
        )

    def rt_all(half):
        return pltpu.make_async_remote_copy(
            src_ref=pbuf.at[half, pl.ds(0, NDOC - 1)], dst_ref=back.at[half, pl.ds(0, NDOC - 1)],
            send_sem=rt_s.at[half], recv_sem=rt_r.at[half], device_id={"doc": sibling}, device_id_type=MESH,
        )

    def rt_copy(half, k):
        peer = lax.rem(doc + k + 1, NDOC)
        return pltpu.make_async_remote_copy(
            src_ref=pbuf.at[half, peer], dst_ref=back.at[half, doc],
            send_sem=rt_s.at[half], recv_sem=rt_r.at[half], device_id={"doc": peer}, device_id_type=MESH,
        )

    def own_copy(half):
        return pltpu.make_async_copy(pbuf.at[half, doc], back.at[half, doc], osem.at[half])

    def give_back(half):
        for k in range(NDOC - 1):
            rt_copy(half, k).start()
        own_copy(half).start()

    def weights_of(half):
        for c0 in range(0, VL, 128):
            part = wall[half, :, :, c0:c0 + 128].reshape(HL, 128)
            wt[c0:c0 + 128, :] = part.T

    def score(half, i, axis):
        first = pl.multiple_of((2 * i + axis) * 4, 4)

        @pl.when(half == 0)
        def _():
            for t in range(4):
                keep = occrow[pl.ds(first + t, 1), :].astype(BF)
                dv[first + t] = dv[first + t] * keep

        docs = dv[pl.ds(first, 4)].reshape(512, VL)
        r = jnp.dot(docs, wt[...], preferred_element_type=F32).reshape(4, NZ, NY, 8, HL)
        for zz in range(NZ):
            for yy in range(NY):
                part = jnp.concatenate([r[t, zz, yy] for t in range(4)], axis=0).astype(BF)
                sbuf[half, axis, i, yy + axis * (zz - yy), zz + axis * (yy - zz)] = part
        for k in (1, 0, 2):
            s1_copy(half, axis, i, k).start()

    def reduce1(half, i, axis):
        s1_all(half, axis, i).wait_recv()
        tot = sbuf[half, axis, i, y + axis * (z - y)].astype(F32)
        for k in range(3):
            tot = tot + rbuf[half, axis, i, k].astype(F32)
        s2buf[half, axis, i] = tot.astype(BF)
        for k in (1, 0, 2):
            s2_copy(half, axis, i, k).start()
        s1_all(half, axis, i).wait_send()

    def reduce2(half, i, axis):
        lane_group = lax.broadcasted_iota(jnp.int32, (8, 128), 1) // HQ
        s2_all(half, axis, i).wait_recv()
        tot = s2buf[half, axis, i, z + axis * (y - z)].astype(F32)
        for k in range(3):
            tot = tot + r2buf[half, axis, i, k].astype(F32)
        for j in range(NDOC):
            made = jnp.zeros((8, 128), F32)
            for t in range(4):
                piece = tot[t * 8:(t + 1) * 8, (j // 4) * 128:(j // 4 + 1) * 128]
                turn = ((t - j % 4) * HQ) % 128
                if turn:
                    piece = pltpu.roll(piece, turn, 1)
                made = jnp.where(lane_group == t, piece, made)
            pbuf[half, j, 2 * i + axis] = made.astype(BF)

    occupancy_rows()
    tw_cp.wait()

    @pl.loop(0, 4)
    def _(c):
        expand(c)

        @pl.when(c == 0)
        def _():
            pltpu.make_async_copy(dwv, dwv, wsem.at[1]).wait()
            pl.semaphore_wait(barrier, NDOC - 1 + 6)
            for b in range(NB):
                d_copy(b).start()

        @pl.when(c >= 2)
        def _():
            ag_pass(c - 2)

        decode(c)

    qw_cp = pltpu.make_async_copy(qw_v, qw_ref, osem.at[2])
    qw_cp.start()
    pltpu.make_async_copy(dv, dv, dsem).wait()

    @pl.loop(0, 2)
    def _(half):
        @pl.when(half == 1)
        def _():
            ag_pass(3)

        ag_wait(2 * half)
        ag_wait(2 * half + 1)
        weights_of(half)

        @pl.loop(0, 4)
        def _(n):
            score(half, n // 2, lax.rem(n, 2))

            @pl.when((half == 0) & (n == 1))
            def _():
                ag_pass(2)

    @pl.loop(0, 8)
    def _(n):
        reduce1(n // 4, lax.rem(n // 2, 2), lax.rem(n, 2))

    @pl.loop(0, 4)
    def _(c):
        ag_sent(c)

    @pl.loop(0, 2)
    def _(half):
        @pl.loop(0, 4)
        def _(n):
            reduce2(half, n // 2, lax.rem(n, 2))

        give_back(half)

    @pl.loop(0, 8)
    def _(n):
        s2_all(n // 4, lax.rem(n, 2), lax.rem(n // 2, 2)).wait_send()

    qw_cp.wait()
    for half in range(2):
        own_copy(half).wait()
        rt_all(half).wait()


def pick(qw_ref, back, cand_ref, qw_out, out_ref, want):
    qw_out[...] = qw_ref[...]
    part = lax.broadcasted_iota(jnp.int32, (CAND, 128), 1) // HQ
    for half in range(2):
        mine = cand_ref[:, half * HQ:(half + 1) * HQ]
        want[half] = jnp.concatenate([mine] * 4, axis=1) - part

    @pl.loop(0, CAND // 8)
    def _(block):
        made = []
        for half in range(2):
            rows = want[half, pl.ds(pl.multiple_of(block * 8, 8), 8), :]
            each = [jnp.broadcast_to(rows[i:i + 1, :], (8, 128)) for i in range(8)]
            accs = [jnp.zeros((8, 128), F32) for _ in range(8)]
            for e in range(NDOC * 4):
                found = back[half, e // 4, e % 4].astype(F32)
                for i in range(8):
                    accs[i] = jnp.where(each[i] == 4 * e, found, accs[i])
            for i in range(8):
                acc = accs[i] + pltpu.roll(accs[i], 64, 1)
                made.append(acc + pltpu.roll(acc, 32, 1))
        for i in range(8):
            out_ref[block * 8 + i, :, 0:HQ] = made[i][:, 0:HQ]
            out_ref[block * 8 + i, :, HQ:2 * HQ] = made[8 + i][:, HQ:2 * HQ]


def body(
    query_states, token_ids, transform_weight, transform_bias, norm_gain, norm_bias,
    decoder_weight, decoder_bias, candidates, occupancy, doc_blocks,
):
    any_ = pl.BlockSpec(memory_space=pl.ANY)
    vm = pl.BlockSpec(memory_space=pltpu.VMEM)
    dma = pltpu.SemaphoreType.DMA
    weights, back = pl.pallas_call(
        kernel,
        out_shape=(
            jax.ShapeDtypeStruct((QD, VL), BF),
            jax.ShapeDtypeStruct((2, NDOC, 4, 8, 128), BF),
        ),
        in_specs=[any_] * 10,
        out_specs=(any_, any_),
        scratch_shapes=[
            pltpu.VMEM((QD, QLEN, DM), BF),
            pltpu.VMEM((DM, DM), BF),
            pltpu.VMEM((DM, VL), BF),
            pltpu.VMEM((NTL, 128, VL), BF),
            pltpu.VMEM((QLEN, QD), jnp.int32),
            pltpu.VMEM((6, 128), F32),
            pltpu.VMEM((6, 128), F32),
            pltpu.VMEM((6, 128), F32),
            pltpu.VMEM((NB, 128), F32),
            pltpu.VMEM((NTL, NB), jnp.int32),
            pltpu.VMEM((NTL, VL), F32),
            pltpu.VMEM((QD, 128), F32),
            pltpu.VMEM((TOK, DM), BF),
            pltpu.VMEM((QD, VL), BF),
            pltpu.VMEM((2, NDOC, HQ, VL), BF),
            pltpu.VMEM((VL, HL), BF),
            pltpu.VMEM((2, 2, 2, 4, 4, 32, HL), BF),
            pltpu.VMEM((2, 2, 2, 3, 4, 32, HL), BF),
            pltpu.VMEM((2, 2, 2, 4, 32, HL), BF),
            pltpu.VMEM((2, 2, 2, 3, 32, HL), BF),
            pltpu.VMEM((2, NDOC, 4, 8, 128), BF),
            dma((4,)),
            dma((2,)),
            dma(()),
            dma((6,)),
            dma((3,)),
            dma((4,)),
            dma((4, 2)),
            dma((2, 2, 2)),
            dma((2, 2, 2)),
            dma((2, 2, 2)),
            dma((2, 2, 2)),
            dma((2,)),
            dma((2,)),
        ],
        compiler_params=pltpu.CompilerParams(
            collective_id=0, has_side_effects=True, vmem_limit_bytes=60 * 1024 * 1024
        ),
        name="splade",
    )(
        query_states, token_ids.T, transform_weight, transform_bias.reshape(6, 128), norm_gain.reshape(6, 128),
        norm_bias.reshape(6, 128), decoder_weight, decoder_bias.reshape(NB, 128), occupancy, doc_blocks,
    )
    weights, picked = pl.pallas_call(
        pick,
        out_shape=(
            jax.ShapeDtypeStruct((QD, VL), BF),
            jax.ShapeDtypeStruct((CAND, 8, QD), F32),
        ),
        in_specs=[vm, vm, vm],
        out_specs=(vm, vm),
        scratch_shapes=[pltpu.VMEM((2, CAND, 128), jnp.int32)],
        name="pick",
    )(weights, back, candidates.T)
    return weights, picked.transpose(2, 0, 1)


def solution(mesh):
    placed = (
        P("doc", None, None),
        P("doc", None),
        P(),
        P(),
        P(),
        P(),
        P(None, "term"),
        P("term"),
        P("doc", None),
        P("doc", "term"),
        P("doc", "term", None, None),
    )
    return jax.shard_map(
        body,
        mesh=mesh,
        in_specs=placed,
        out_specs=(P("doc", "term"), P("doc", None, "term")),
        check_vma=False,
    )
```
